32 devices in a mesh: grp: 2 (over x), chan: 16 (over z, y, core).
Axes of the slice: x: 2, y: 2, z: 4, core: 2. Of those that a mesh axis runs over, the one named last changes fastest.
Arguments:
- traces: bfloat16 [32, 16, 256, 512], P(('grp', 'chan')), parts along dimension 0, may hold values from -6 to 6
- mask: int32 [32, 16], P('grp'), parts along dimension 0, may hold values 0 or 1
- counts: int32 [32], P('grp'), parts along dimension 0, may hold values from 0 to 5, as said below
Outputs:
- forward: float32 [32, 5, 128, 512], P(('grp', 'chan')), parts along dimension 0
- backward: float32 [32, 5, 128, 512], P(('grp', 'chan')), parts along dimension 0
The draws below stay inside these ranges and needn't reach their ends.
There are 2 independent parts, one for each index of `grp`. The reference program is written for one: setup_inputs(seed, part) draws one part's arguments, and reference() takes and returns one part's arrays. A program takes and returns all parts, laid end to end along the dimension named above; each array names one. Nothing has to cross between parts.
Inputs may be any that keep to these rules, and one draw needn't show every extreme that they name: counts[b] <= min(5, 15 - b); block 0 always has 5 partners.
All inputs are finite; a program needn't handle non-finite values.
Results may differ from the reference program's by a relative error of at most 0.0063.
Values may be sent and summed in bfloat16 or wider, within the bound.
A program may use at most 128 MiB of HBM per device.

```python
import math
import jax
import jax.numpy as jnp
from jax import lax

CH = 512
L = 256
W = 16
MAXP = 5
BLOCKS = 16


def draw_counts(key, part):
    blocks = jnp.arange(BLOCKS, dtype=jnp.int32)
    drawn = jax.random.randint(key, (BLOCKS,), 1, MAXP + 1).astype(jnp.int32)
    drawn = jnp.where(blocks == 0, MAXP, drawn)
    return jnp.minimum(drawn, BLOCKS - 1 - blocks).astype(jnp.int32)


def with_ends(entries, stream_key, smallest, high):
    spot = [jax.random.randint(jax.random.fold_in(stream_key, axis), (), 0, length) for axis, length in enumerate(entries.shape)]
    widest = entries.shape.index(max(entries.shape))
    neighbour = spot[:widest] + [(spot[widest] + 1) % entries.shape[widest]] + spot[widest + 1:]
    return entries.at[tuple(spot)].set(smallest).at[tuple(neighbour)].set(high)


def levels(key, extent, shards, low, top_value):
    def one(axis_at, blocks):
        heights = jax.random.uniform(jax.random.fold_in(jax.random.fold_in(key, 6), axis_at), (blocks,), jnp.float32, low / len(shards), top_value / len(shards))
        return jnp.repeat(jnp.exp(heights), extent[axis_at] // blocks).reshape((-1,) + (1,) * (len(extent) - axis_at - 1))

    loudness = one(*shards[0])
    for cut in shards[1:]:
        loudness = loudness * one(*cut)
    return loudness


def noise(key, dims, scale, limit, split=(), kind=jnp.bfloat16):
    factor_of = levels(key, dims, split, -0.22, 0.18) if split else 1.0
    values = jax.random.normal(key, dims, jnp.float32) * scale * factor_of
    return jnp.minimum(jnp.maximum(values, -limit), limit).astype(kind)


def setup_inputs(seed: int = 0, part: int = 0) -> dict:
    keys = jax.random.split(jax.random.key(seed), 4)
    part_keys = jax.random.split(jax.random.fold_in(keys[3], part), 4)
    traces = noise(part_keys[0], (BLOCKS, W, L, CH), 1.0, 6.0, ((0, 16),))
    mask = with_ends((jax.random.randint(part_keys[1], (BLOCKS, W), 0, 4) < 3).astype(jnp.int32), jax.random.fold_in(part_keys[1], 1), 0, 1)
    counts = draw_counts(jax.random.fold_in(jax.random.fold_in(keys[3], part), 71), part)
    return dict(traces=traces, mask=mask, counts=counts)


def lag_table(lags, bins):
    times = jnp.arange(lags, dtype=jnp.int32)[:, None]
    freqs = jnp.arange(1, bins + 1, dtype=jnp.int32)[None, :]
    phase = (times * freqs % lags).astype(jnp.float32) * (2.0 * math.pi / lags)
    return jnp.concatenate([jnp.cos(phase), -jnp.sin(phase)], axis=1).astype(jnp.bfloat16)

def whiten(record, table):
    bins = table.shape[1] // 2
    raw = jnp.einsum('tk,wtc->wkc', table.astype(jnp.float32), record.astype(jnp.float32), precision=lax.Precision.HIGHEST)
    power = lax.optimization_barrier(jnp.sum(raw * raw, axis=1)) / bins
    return (raw / jnp.sqrt(power + 1e-06)[:, None, :]).astype(jnp.bfloat16)

def stack_pair(first, second, weight):
    half = first.shape[1] // 2
    wlen = first.shape[0]
    first_re = first[:, :half].astype(jnp.float32)
    first_im = first[:, half:].astype(jnp.float32)
    second_re = second[:, :half].astype(jnp.float32)
    second_im = second[:, half:].astype(jnp.float32)
    scaled = weight[:, None, None]
    real_part = lax.optimization_barrier(jnp.sum(scaled * (first_re * second_re + first_im * second_im), axis=0))
    imag_part = lax.optimization_barrier(jnp.sum(scaled * (first_im * second_re - first_re * second_im), axis=0))
    return (jnp.concatenate([real_part, imag_part], axis=0) / math.sqrt(wlen)).astype(jnp.bfloat16)

def pair_lags(first, second, weight, table, bins):
    stacked = stack_pair(first, second, weight)
    return jnp.dot(table, stacked, preferred_element_type=jnp.float32) / math.sqrt(bins)

def reference(traces, mask, counts):
    blocks = traces.shape[0]
    lags = traces.shape[2]
    bins = lags // 2
    table = lag_table(lags, bins)
    white = lax.map(lambda record: whiten(record, table), traces)
    valid = mask.astype(jnp.float32)

    def one_block(block):
        causal = []
        acausal = []
        for step in range(1, MAXP + 1):
            other = jnp.minimum(block + step, blocks - 1).astype(jnp.int32)
            weight = valid[block] * valid[other]
            corr = pair_lags(white[block], white[other], weight, table, bins)
            corr = jnp.where(counts[block] >= step, corr, jnp.zeros_like(corr))
            causal.append(corr[:bins])
            acausal.append(corr[bins:][::-1])
        return (jnp.stack(causal), jnp.stack(acausal))
    forward, acausal_all = lax.map(one_block, jnp.arange(blocks, dtype=jnp.int32))
    rows = jnp.arange(blocks, dtype=jnp.int32)
    backward_list = []
    for step in range(1, MAXP + 1):
        rolled = jnp.roll(acausal_all[:, step - 1], step, axis=0)
        backward_list.append(jnp.where((rows >= step)[:, None, None], rolled, jnp.zeros_like(rolled)))
    backward = jnp.stack(backward_list, axis=1)
    return (forward, backward)
```

```python
import functools
import math

import numpy as np

import jax
import jax.numpy as jnp
from jax import lax
from jax.experimental import pallas as pl
from jax.experimental.pallas import tpu as pltpu
from jax.sharding import PartitionSpec as P

MAXP = 5
TEAM = 4
LANES = 128
GROUPS = 4
SLOTS = 9
TILE = 32
SPAN = 5

OWN_PAIRS = [(2, 3, 3), (3, 4, 2), (4, 5, 1)]
A_PAIRS = [(0, 2, 4), (1, 2, 4)]
B_PAIRS = [(2, 6, 2), (3, 6, 2)]
C_PAIRS = [(3, 8, 1)]
AB_PAIRS = [(1, 6, 1)]
FIRST = {}
for _runs in (OWN_PAIRS, A_PAIRS, B_PAIRS, C_PAIRS, AB_PAIRS):
    for _run in _runs:
        FIRST[_run] = sum(r[2] for r in FIRST)
PAIRS = sum(r[2] for r in FIRST)


def lag_table(lags, bins):
    times = np.arange(lags, dtype=np.int32)[:, None]
    freqs = np.arange(1, bins + 1, dtype=np.int32)[None, :]
    phase = (times * freqs % lags).astype(np.float32) * np.float32(2.0 * math.pi / lags)
    return np.concatenate([np.cos(phase), -np.sin(phase)], axis=1)


def kernel(axis, n, traces, mask_in, counts_in, table_t_in, table_lag_in, back,
           mask, counts, table_t, table_lag, fetch, record, white, acc, res, t_send, t_recv, z_send, z_recv, r_send, r_recv):
    me = lax.axis_index(axis)
    team = me // TEAM
    q = me % TEAM
    base = team * TEAM
    odd = q % 2
    teams = n // TEAM
    wins = record.shape[1]
    lags = record.shape[2]
    bins = lags // 2
    chunk = wins // GROUPS
    below = team > 0
    above = team < teams - 1
    step = TEAM * (1 - 2 * odd)
    has_a = jnp.where(odd == 0, team, teams - 1 - team) > 0
    has_b = jnp.where(odd == 0, teams - 1 - team, team) > 0
    sign = (1 - 2 * odd).astype(jnp.float32)

    def block_of(slot):
        return base + jnp.where(odd == 0, slot - 2, 5 - slot)

    fetches = [
        pltpu.make_async_copy(src, dst, fetch.at[k])
        for k, (src, dst) in enumerate(
            ((table_t_in, table_t), (mask_in, mask), (table_lag_in, table_lag), (counts_in, counts)))
    ]
    for copy in fetches:
        copy.start()
    early_low = (q % 3) == 0
    first = jnp.where(early_low, 0, 2)
    barrier = pltpu.get_barrier_semaphore()
    for shift in (-1, 0, 1):
        for i in range(TEAM):
            other = base + shift * TEAM + i
            there = (other >= 0) & (other < n) & (other != me)

            @pl.when(there)
            def _():
                pl.semaphore_signal(barrier, inc=1, device_id={axis: other})

    def windows(g):
        return pl.ds(g * chunk, chunk)

    def lanes(i):
        return pl.ds(pl.multiple_of(i * LANES, LANES), LANES)

    def trace_copy(peer, g):
        return pltpu.make_async_remote_copy(
            src_ref=traces.at[0, windows(g), :, lanes(peer)],
            dst_ref=record.at[q, windows(g)],
            send_sem=t_send.at[peer, g],
            recv_sem=t_recv.at[q, g],
            device_id={axis: base + peer},
        )

    def own_copy(g):
        return pltpu.make_async_copy(traces.at[0, windows(g), :, lanes(q)], record.at[q, windows(g)], t_recv.at[q, g])

    peers = ((q + 2) % TEAM, 3 - q, q + 1 - 2 * odd)
    for g in range(GROUPS):
        own_copy(g).start()

    def to_a(u, g):
        return pltpu.make_async_remote_copy(
            src_ref=white.at[u + 2, windows(g)],
            dst_ref=white.at[u + 6, windows(g)],
            send_sem=z_send.at[u, g],
            recv_sem=z_recv.at[u + 2, g],
            device_id={axis: me - step},
        )

    def to_b(u, g):
        return pltpu.make_async_remote_copy(
            src_ref=white.at[u + 2, windows(g)],
            dst_ref=white.at[u - 2, windows(g)],
            send_sem=z_send.at[u + 1, g],
            recv_sem=z_recv.at[u - 2, g],
            device_id={axis: me + step},
        )

    own_slot = jnp.where(odd == 0, q, 3 - q)

    def whiten_block(u, g):
        i = jnp.where(odd == 0, u, 3 - u)
        pltpu.make_async_copy(record.at[i, windows(g)], record.at[i, windows(g)], t_recv.at[i, g]).wait()
        for h in range(0, chunk, 2):
            w = g * chunk + h
            rec = jnp.concatenate([record[i, w], record[i, w + 1]], axis=1)
            raw = jnp.dot(table_t[...], rec, preferred_element_type=jnp.float32)
            power = jnp.sum(raw * raw, axis=0, keepdims=True) / bins
            inv = 1.0 / jnp.sqrt(power + 1e-06)
            for e in range(2):
                part = slice(e * LANES, (e + 1) * LANES)
                keep = mask[base + i, w + e].astype(jnp.float32)
                white[u + 2, w + e] = (raw[:, part] * (inv[:, part] * keep)).astype(jnp.bfloat16)

    def pass_on(u, g):
        @pl.when((u <= 2) & has_a)
        def _():
            to_a(u, g).start()

        @pl.when((u >= 2) & has_b)
        def _():
            to_b(u, g).start()

    def block_chunks(u, start):
        def one(g, carry):
            whiten_block(u, g)
            pass_on(u, g)
            return carry

        lax.fori_loop(start, GROUPS, one, 0)

    def stack_run(run, g):
        s, t0, count = run
        place = FIRST[run]

        def one(v, carry):
            t = t0 + v

            def tile(k, inner):
                re_at = pl.ds(pl.multiple_of(k * TILE, TILE), TILE)
                im_at = pl.ds(pl.multiple_of(bins + k * TILE, TILE), TILE)
                fresh = g == 0
                real = jnp.where(fresh, 0.0, acc[place + v, re_at, :])
                imag = jnp.where(fresh, 0.0, acc[place + v, im_at, :])
                for h in range(chunk):
                    w = g * chunk + h
                    a_re = white[s, w, re_at, :].astype(jnp.float32)
                    a_im = white[s, w, im_at, :].astype(jnp.float32)
                    b_re = white[t, w, re_at, :].astype(jnp.float32)
                    b_im = white[t, w, im_at, :].astype(jnp.float32)
                    real = real + (a_re * b_re + a_im * b_im)
                    imag = imag + (a_im * b_re - a_re * b_im)
                acc[place + v, re_at, :] = real
                acc[place + v, im_at, :] = imag
                return inner

            lax.fori_loop(0, bins // TILE, tile, 0)
            return carry

        lax.fori_loop(0, count, one, 0)

    def result_copies(s, t, index):
        early = block_of(jnp.where(odd == 0, s, t))
        late = block_of(jnp.where(odd == 0, t, s))
        out = []
        for side, owner in ((0, early), (1, late)):
            src = res.at[index, pl.ds(side * bins, bins)]
            dst = back.at[side, t - s - 1, :, lanes(q)]
            local = pltpu.make_async_copy(src, dst, r_recv.at[side, t - s - 1])
            remote = pltpu.make_async_remote_copy(
                src_ref=src, dst_ref=dst, send_sem=r_send.at[index, side],
                recv_sem=r_recv.at[side, t - s - 1], device_id={axis: owner},
            )
            out.append((owner, local, remote))
        return out

    def finish_run(run):
        s, t0, count = run
        place = FIRST[run]

        def one(v, carry):
            total = acc[place + v] * (1.0 / math.sqrt(wins))
            stacked = jnp.concatenate([total[:bins], total[bins:] * sign], axis=0).astype(jnp.bfloat16)
            corr = jnp.dot(table_lag[...], stacked, preferred_element_type=jnp.float32) * (1.0 / math.sqrt(bins))
            early = block_of(jnp.where(odd == 0, s, t0 + v))
            reach = counts[early] >= t0 + v - s
            res[place + v] = jnp.where(reach, corr, 0.0).astype(jnp.bfloat16)
            for owner, local, remote in result_copies(s, t0 + v, place + v):
                @pl.when(owner == me)
                def _():
                    local.start()

                @pl.when(owner != me)
                def _():
                    remote.start()
            return carry

        lax.fori_loop(0, count, one, 0)

    def finish_sends(run):
        s, t0, count = run
        place = FIRST[run]

        def one(v, carry):
            for owner, local, remote in result_copies(s, t0 + v, place + v):
                @pl.when(owner != me)
                def _():
                    remote.wait_send()
            return carry

        lax.fori_loop(0, count, one, 0)

    def arrived(z, slot, g):
        view = white.at[slot, windows(g)]
        pltpu.make_async_copy(view, view, z_recv.at[z, g]).wait()

    def far(g, carry):
        for v in range(2):
            whiten_block(2 - first + v, g)
            pass_on(2 - first + v, g)
        for run in OWN_PAIRS:
            stack_run(run, g)
        return carry

    for copy in fetches[:2]:
        copy.wait()
    whiten_block(own_slot, 0)
    pl.semaphore_wait(barrier, TEAM - 1 + TEAM * below.astype(jnp.int32) + TEAM * above.astype(jnp.int32))
    pass_on(own_slot, 0)
    for g in range(GROUPS):
        for peer in peers:
            trace_copy(peer, g).start()
    block_chunks(own_slot, 1)
    block_chunks(2 * first + 1 - own_slot, 0)
    lax.fori_loop(0, GROUPS, far, 0)
    fetches[2].wait()
    fetches[3].wait()
    for j in range(MAXP):
        for side, gone in ((0, me + j + 1 >= n), (1, me - j - 1 < 0)):
            @pl.when(gone)
            def _():
                back[side, j] = jnp.zeros_like(back[side, j])
    for run in OWN_PAIRS:
        finish_run(run)

    def group(ready, zs, runs):
        @pl.when(ready)
        def _():
            def one(g, carry):
                for z in zs:
                    arrived(z, z if z < 2 else z + 4, g)
                for run in runs:
                    stack_run(run, g)

                    @pl.when(g == GROUPS - 1)
                    def _():
                        finish_run(run)
                return carry

            lax.fori_loop(0, GROUPS, one, 0)

    def half(p, carry):
        low = (p == 0) == early_low
        group(low & has_b, (2, 3), B_PAIRS)
        group(jnp.logical_not(low) & has_a, (0, 1), A_PAIRS)
        group(jnp.logical_not(low) & has_b, (4,), C_PAIRS)
        return carry

    lax.fori_loop(0, 2, half, 0)
    group(has_a & has_b, (), AB_PAIRS)

    def sent(g, carry):
        for peer in peers:
            trace_copy(peer, g).wait_send()

        @pl.when(has_a)
        def _():
            for u in range(3):
                to_a(u, g).wait_send()

        @pl.when(has_b)
        def _():
            for u in range(2, 4):
                to_b(u, g).wait_send()

        return carry

    lax.fori_loop(0, GROUPS, sent, 0)
    for j in range(MAXP):
        for side, there in ((0, me + j + 1 < n), (1, me - j - 1 >= 0)):
            @pl.when(there)
            def _():
                view = back.at[side, j]
                pltpu.make_async_copy(view, view, r_recv.at[side, j]).wait()
    for run in OWN_PAIRS:
        finish_sends(run)

    @pl.when(has_a)
    def _():
        for run in A_PAIRS:
            finish_sends(run)

    @pl.when(has_b)
    def _():
        for run in B_PAIRS + C_PAIRS:
            finish_sends(run)

    @pl.when(has_a & has_b)
    def _():
        for run in AB_PAIRS:
            finish_sends(run)


def widen(back, fwd_out, bwd_out, wide, sems):
    copies = []
    for j in range(MAXP):
        for side, out in ((0, fwd_out), (1, bwd_out)):
            wide[side, j] = back[side, j].astype(jnp.float32)
            copy = pltpu.make_async_copy(wide.at[side, j], out.at[0, j], sems.at[side, j])
            copy.start()
            copies.append(copy)
    for copy in copies:
        copy.wait()


def local(traces, mask, counts):
    axis = "chan"
    n = lax.axis_size(axis)
    _, wins, lags, width = traces.shape
    bins = lags // 2
    table = lag_table(lags, bins)
    table_lag = np.concatenate([table[:bins], table[bins:][::-1]], axis=0)
    lagged = pl.pallas_call(
        functools.partial(kernel, axis, n),
        out_shape=pltpu.VMEM((2, MAXP, bins, width), jnp.bfloat16),
        in_specs=[pl.BlockSpec(memory_space=pltpu.HBM)] * 5,
        out_specs=pl.BlockSpec(memory_space=pltpu.VMEM),
        scratch_shapes=[
            pltpu.SMEM(mask.shape, jnp.int32),
            pltpu.SMEM(counts.shape, jnp.int32),
            pltpu.VMEM((lags, lags), jnp.bfloat16),
            pltpu.VMEM((lags, lags), jnp.bfloat16),
            pltpu.SemaphoreType.DMA((4,)),
            pltpu.VMEM((TEAM, wins, lags, LANES), jnp.bfloat16),
            pltpu.VMEM((SLOTS, wins, lags, LANES), jnp.bfloat16),
            pltpu.VMEM((PAIRS, lags, LANES), jnp.float32),
            pltpu.VMEM((PAIRS, lags, LANES), jnp.bfloat16),
            pltpu.SemaphoreType.DMA((TEAM, GROUPS)),
            pltpu.SemaphoreType.DMA((TEAM, GROUPS)),
            pltpu.SemaphoreType.DMA((5, GROUPS)),
            pltpu.SemaphoreType.DMA((5, GROUPS)),
            pltpu.SemaphoreType.DMA((PAIRS, 2)),
            pltpu.SemaphoreType.DMA((2, MAXP)),
        ],
        compiler_params=pltpu.CompilerParams(collective_id=0, has_side_effects=True, vmem_limit_bytes=40 << 20),
        name="xcorr",
    )(*(pltpu.with_memory_space_constraint(x, pltpu.HBM) for x in (
        traces, mask, counts, jnp.asarray(table.T, jnp.bfloat16), jnp.asarray(table_lag, jnp.bfloat16))))
    wide = jax.ShapeDtypeStruct((1, MAXP, bins, width), jnp.float32)
    return pl.pallas_call(
        widen,
        out_shape=(wide, wide),
        in_specs=[pl.BlockSpec(memory_space=pltpu.VMEM)],
        out_specs=[pl.BlockSpec(memory_space=pltpu.HBM)] * 2,
        scratch_shapes=[
            pltpu.VMEM((2, MAXP, bins, width), jnp.float32),
            pltpu.SemaphoreType.DMA((2, MAXP)),
        ],
        name="widen",
    )(pltpu.with_memory_space_constraint(lagged, pltpu.VMEM))


def solution(mesh):
    return jax.shard_map(
        local,
        mesh=mesh,
        in_specs=(P(("grp", "chan"), None, None, None), P("grp", None), P("grp")),
        out_specs=(P(("grp", "chan"), None, None, None), P(("grp", "chan"), None, None, None)),
        check_vma=False,
    )
```

```python
import functools
import math

import numpy as np

import jax
import jax.numpy as jnp
from jax import lax
from jax.experimental import pallas as pl
from jax.experimental.pallas import tpu as pltpu
from jax.sharding import PartitionSpec as P

MAXP = 5
TEAM = 4
LANES = 128
CHUNK = 2
SLOTS = 9
TILE = 16
LAG = 2
AHEAD = 4
OWN, BELOW, ABOVE, BOTH = range(4)

SOON = [
    ("n0", "n1", OWN), ("n0", "f0", OWN), ("n1", "f0", OWN),
    (0, "n0", BELOW), (0, "n1", BELOW), (0, "f0", BELOW),
    (2, 6, ABOVE), (3, 6, ABOVE),
]
LATE = [
    ("n0", "f1", OWN), ("n1", "f1", OWN), ("f0", "f1", OWN),
    (0, "f1", BELOW), (1, "n0", BELOW), (1, "n1", BELOW), (1, "f0", BELOW), (1, "f1", BELOW),
    (2, 7, ABOVE), (3, 7, ABOVE), (1, 6, BOTH),
]
LAST = (3, 8, ABOVE)
PAIRS = len(SOON) + len(LATE) + 1


def lag_table(lags, bins):
    times = np.arange(lags, dtype=np.int32)[:, None]
    freqs = np.arange(1, bins + 1, dtype=np.int32)[None, :]
    phase = (times * freqs % lags).astype(np.float32) * np.float32(2.0 * math.pi / lags)
    return np.concatenate([np.cos(phase), -np.sin(phase)], axis=1)


def kernel(axis, n, traces, mask_in, counts_in, table_t_in, table_lag_in, back,
           mask, counts, table_t, table_lag, fetch, record, white, acc, res,
           t_send, t_recv, z_send, z_recv, r_send, r_recv):
    me = lax.axis_index(axis)
    team = me // TEAM
    q = me % TEAM
    base = team * TEAM
    odd = q % 2
    teams = n // TEAM
    wins = record.shape[1]
    lags = record.shape[2]
    bins = lags // 2
    groups = wins // CHUNK
    below = team > 0
    above = team < teams - 1
    step = TEAM * (1 - 2 * odd)
    has_a = jnp.where(odd == 0, team, teams - 1 - team) > 0
    has_b = jnp.where(odd == 0, teams - 1 - team, team) > 0
    low = (q % 3) == 0
    sign = (1 - 2 * odd).astype(jnp.float32)
    near_u = jnp.where(low, 0, 2)
    far_u = 2 - near_u
    slot_of = {"n0": near_u + 2, "n1": near_u + 3, "f0": far_u + 2, "f1": far_u + 3}

    def slot(name):
        return slot_of[name] if isinstance(name, str) else name

    def swapped(pair):
        return isinstance(pair[0], str) and pair[0][0] != pair[1][0]

    def there(group):
        return {OWN: True, BELOW: has_a, ABOVE: has_b, BOTH: has_a & has_b}[group]

    def block_of(s):
        return base + jnp.where(odd == 0, s - 2, 5 - s)

    fetches = [
        pltpu.make_async_copy(src, dst, fetch.at[k])
        for k, (src, dst) in enumerate(
            ((table_t_in, table_t), (mask_in, mask), (table_lag_in, table_lag), (counts_in, counts)))
    ]
    barrier = pltpu.get_barrier_semaphore()
    for shift in (0, -1, 1):
        for i in range(TEAM):
            other = base + shift * TEAM + i

            @pl.when((other >= 0) & (other < n) & (other != me))
            def _():
                pl.semaphore_signal(barrier, inc=1, device_id={axis: other})

    for copy in fetches:
        copy.start()

    def windows(g):
        return pl.ds(g * CHUNK, CHUNK)

    def lanes(i):
        return pl.ds(pl.multiple_of(i * LANES, LANES), LANES)

    def trace_copy(peer, at):
        return lambda g: pltpu.make_async_remote_copy(
            src_ref=traces.at[0, at(g), :, lanes(peer)],
            dst_ref=record.at[q, at(g)],
            send_sem=t_send.at[peer],
            recv_sem=t_recv.at[q, g],
            device_id={axis: base + peer},
        )

    def own_copy(g):
        return pltpu.make_async_copy(traces.at[0, windows(g), :, lanes(q)], record.at[q, windows(g)], t_recv.at[q, g])

    peers = (q + 1 - 2 * odd, (q + 2) % TEAM, 3 - q)
    for g in range(groups):
        own_copy(g).start()

    def every(g):
        return pl.ds(0, wins)

    def to_a(u, g, at=windows):
        return pltpu.make_async_remote_copy(
            src_ref=white.at[u + 2, at(g)],
            dst_ref=white.at[u + 6, at(g)],
            send_sem=z_send.at[u],
            recv_sem=z_recv.at[u + 2, g],
            device_id={axis: me - step},
        )

    def to_b(u, g, at=windows):
        return pltpu.make_async_remote_copy(
            src_ref=white.at[u + 2, at(g)],
            dst_ref=white.at[u - 2, at(g)],
            send_sem=z_send.at[u + 1],
            recv_sem=z_recv.at[u - 2, g],
            device_id={axis: me + step},
        )

    def whiten_block(u, g):
        i = jnp.where(odd == 0, u, 3 - u)
        pltpu.make_async_copy(record.at[i, windows(g)], record.at[i, windows(g)], t_recv.at[i, g]).wait()
        w = g * CHUNK
        rec = jnp.concatenate([record[i, w + e] for e in range(CHUNK)], axis=1)
        raw = jnp.dot(table_t[...], rec, preferred_element_type=jnp.float32)
        power = jnp.sum(raw * raw, axis=0, keepdims=True) / bins
        inv = 1.0 / jnp.sqrt(power + 1e-06)
        for e in range(CHUNK):
            part = slice(e * LANES, (e + 1) * LANES)
            keep = mask[base + i, w + e].astype(jnp.float32)
            white[u + 2, w + e] = (raw[:, part] * (inv[:, part] * keep)).astype(jnp.bfloat16)

    def send_a(u, g):
        @pl.when(has_a)
        def _():
            to_a(u, g).start()

    def send_b(u, g):
        @pl.when(has_b)
        def _():
            to_b(u, g).start()

    def arrived(z, g):
        view = white.at[z if z < 2 else z + 4, windows(g)]
        pltpu.make_async_copy(view, view, z_recv.at[z, g]).wait()

    place_of = {pair[:2]: k for k, pair in enumerate(SOON + LATE + [LAST])}

    def stack(pairs, g):
        def tile(k, carry):
            re_at = pl.ds(pl.multiple_of(k * TILE, TILE), TILE)
            im_at = pl.ds(pl.multiple_of(bins + k * TILE, TILE), TILE)
            sums = [(acc[place_of[p[:2]], re_at, :], acc[place_of[p[:2]], im_at, :]) for p in pairs]
            for h in range(CHUNK):
                w = g * CHUNK + h
                names = list(dict.fromkeys(name for p in pairs for name in p[:2]))
                held = {
                    name: (white[slot(name), w, re_at, :].astype(jnp.float32), white[slot(name), w, im_at, :].astype(jnp.float32))
                    for name in names
                }
                for k2, p in enumerate(pairs):
                    a_re, a_im = held[p[0]]
                    b_re, b_im = held[p[1]]
                    real, imag = sums[k2]
                    sums[k2] = (real + (a_re * b_re + a_im * b_im), imag + (a_im * b_re - a_re * b_im))
            for k2, p in enumerate(pairs):
                acc[place_of[p[:2]], re_at, :] = sums[k2][0]
                acc[place_of[p[:2]], im_at, :] = sums[k2][1]
            return carry

        lax.fori_loop(0, bins // TILE, tile, 0)

    def result_copies(s, t, place, group):
        early = block_of(jnp.where(odd == 0, s, t))
        late = block_of(jnp.where(odd == 0, t, s))
        out = []
        for side, owner in ((0, early), (1, late)):
            src = res.at[2 * place + side]
            dst = back.at[side, t - s - 1, :, lanes(q)]
            local = pltpu.make_async_copy(src, dst, r_recv.at[side, t - s - 1])
            remote = pltpu.make_async_remote_copy(
                src_ref=src, dst_ref=dst, send_sem=r_send.at[group],
                recv_sem=r_recv.at[side, t - s - 1], device_id={axis: owner},
            )
            out.append((owner, local, remote))
        return early, out

    def finish(place, first, second, group):
        s = jnp.minimum(first, second)
        t = jnp.maximum(first, second)
        turn = jnp.where(first < second, sign, -sign)
        early, copies = result_copies(s, t, place, group)
        total = acc[place] * (1.0 / math.sqrt(wins))
        stacked = jnp.concatenate([total[:bins], total[bins:] * turn], axis=0).astype(jnp.bfloat16)
        corr = jnp.dot(table_lag[...], stacked, preferred_element_type=jnp.float32) * (1.0 / math.sqrt(bins))
        corr = jnp.where(counts[early] >= t - s, corr, 0.0).astype(jnp.bfloat16)
        res[2 * place] = corr[:bins]
        res[2 * place + 1] = corr[bins:]
        for owner, local, remote in copies:
            @pl.when(owner == me)
            def _():
                local.start()

            @pl.when(owner != me)
            def _():
                remote.start()

    def choose(k, values):
        out = values[0]
        for at, value in enumerate(values[1:], 1):
            out = jnp.where(k == at, value, out)
        return out

    def finish_listed(k, pairs, first_place, skip):
        wanted = [jnp.asarray(there(p[2])) for p in pairs]
        if skip is not None:
            wanted[skip[0]] = wanted[skip[0]] & skip[1]

        ready = choose(k, [jnp.where(x, 1, 0) for x in wanted]) > 0

        @pl.when(ready)
        def _():
            finish(first_place(k), choose(k, [slot(p[0]) for p in pairs]), choose(k, [slot(p[1]) for p in pairs]),
                   choose(k, [p[2] for p in pairs]))

    for copy in fetches[:2]:
        copy.wait()
    own_u = near_u
    whiten_block(own_u, 0)
    pl.semaphore_wait(barrier, TEAM - 1 + TEAM * below.astype(jnp.int32) + TEAM * above.astype(jnp.int32))

    def start_own(g):
        @pl.when(low)
        def _():
            send_a(0, g)

        @pl.when(jnp.logical_not(low))
        def _():
            send_b(2, g)

            @pl.when(g < AHEAD)
            def _():
                send_a(2, g)

    start_own(0)
    for peer in peers:
        copy = trace_copy(peer, windows)
        for g in range(groups):
            copy(g).start()

    def own_chunk(g, carry):
        whiten_block(own_u, g)
        start_own(g)
        return carry

    lax.fori_loop(1, groups, own_chunk, 0)
    acc[...] = jnp.zeros_like(acc)
    for j in range(MAXP):
        for side, gone in ((0, me + j + 1 >= n), (1, me - j - 1 < 0)):
            @pl.when(gone)
            def _():
                back[side, j] = jnp.zeros_like(back[side, j])
    for copy in fetches[2:]:
        copy.wait()

    soon_own = [p for p in SOON if p[2] == OWN]
    soon_a = [p for p in SOON if p[2] == BELOW]
    late_own = [p for p in LATE if p[2] == OWN]
    late_a = [p for p in LATE if p[2] == BELOW]

    def one_step(k, carry):
        late = k >= groups
        g = jnp.where(late, k - groups, k)

        @pl.when(k < 2 * groups)
        def _():
            u = far_u + late.astype(jnp.int32)
            whiten_block(u, g)

            @pl.when(low)
            def _():
                send_b(u, g)

                @pl.when(late)
                def _():
                    send_a(2, g)

            @pl.when(jnp.logical_not(low))
            def _():
                send_a(u, g)

        @pl.when(k < groups)
        def _():
            u = near_u + 1
            whiten_block(u, g)

            @pl.when(low)
            def _():
                send_a(u, g)

            @pl.when(jnp.logical_not(low))
            def _():
                send_b(u, g)

            stack(soon_own, g)

        @pl.when(late & (k < 2 * groups))
        def _():
            stack(late_own, g)

        @pl.when((k == 2 * groups) & jnp.logical_not(low))
        def _():
            for h in range(AHEAD, groups):
                send_a(2, h)

        @pl.when((k >= LAG) & (k < groups + LAG))
        def _():
            h = k - LAG

            @pl.when(has_a)
            def _():
                arrived(0, h)
                stack(soon_a, h)

            @pl.when(has_b)
            def _():
                arrived(2, h)
                stack([(2, 6)], h)

                @pl.when(low)
                def _():
                    stack([(3, 6)], h)

        @pl.when(k >= groups + LAG)
        def _():
            h = k - groups - LAG

            @pl.when(has_a)
            def _():
                arrived(1, h)
                stack([p for p in late_a if p[0] == 0], h)
                stack([p for p in late_a if p[0] == 1], h)

            @pl.when(has_b)
            def _():
                arrived(3, h)
                stack([(2, 7), (3, 7)], h)

                @pl.when(jnp.logical_not(low))
                def _():
                    stack([(3, 6)], h)

            @pl.when(has_a & has_b)
            def _():
                stack([(1, 6)], h)

            finish_listed(h, SOON, lambda i: i, (7, low))

        return carry

    lax.fori_loop(0, 2 * groups + LAG, one_step, 0)

    final = LATE + [(3, 6, ABOVE)]

    def finish_late(k, carry):
        finish_listed(k, final, lambda i: jnp.where(i == len(LATE), 7, i + len(SOON)), (len(LATE), jnp.logical_not(low)))
        return carry

    lax.fori_loop(0, len(final), finish_late, 0)

    @pl.when(has_b)
    def _():
        def last(g, carry):
            arrived(4, g)
            stack([LAST], g)
            return carry

        lax.fori_loop(0, groups, last, 0)
        finish(place_of[LAST[:2]], 3, 8, ABOVE)

    for peer in peers:
        trace_copy(peer, every)(0).wait_send()

    @pl.when(has_a)
    def _():
        for u in range(3):
            to_a(u, 0, every).wait_send()

    @pl.when(has_b)
    def _():
        for u in range(2, 4):
            to_b(u, 0, every).wait_send()

    def results_sent(group, count, when):
        @pl.when(when)
        def _():
            view = res.at[pl.ds(0, count)]
            pltpu.make_async_copy(view, view, r_send.at[group]).wait()

    results_sent(OWN, 9, me >= 0)
    results_sent(BELOW, 14, has_a)
    results_sent(ABOVE, 8, has_b & low)
    results_sent(ABOVE, 10, has_b & jnp.logical_not(low))
    results_sent(BOTH, 2, has_a & has_b)
    for j in range(MAXP):
        for side, some in ((0, me + j + 1 < n), (1, me - j - 1 >= 0)):
            @pl.when(some)
            def _():
                view = back.at[side, j]
                pltpu.make_async_copy(view, view, r_recv.at[side, j]).wait()


def widen(back, fwd_out, bwd_out, wide, sems):
    copies = []
    for j in range(MAXP):
        for side, out in ((0, fwd_out), (1, bwd_out)):
            wide[side, j] = back[side, j].astype(jnp.float32)
            copy = pltpu.make_async_copy(wide.at[side, j], out.at[0, j], sems.at[side, j])
            copy.start()
            copies.append(copy)
    for copy in copies:
        copy.wait()


def local(traces, mask, counts):
    axis = "chan"
    n = lax.axis_size(axis)
    _, wins, lags, width = traces.shape
    bins = lags // 2
    groups = wins // CHUNK
    table = lag_table(lags, bins)
    table_lag = np.concatenate([table[:bins], table[bins:][::-1]], axis=0)
    lagged = pl.pallas_call(
        functools.partial(kernel, axis, n),
        out_shape=pltpu.VMEM((2, MAXP, bins, width), jnp.bfloat16),
        in_specs=[pl.BlockSpec(memory_space=pltpu.HBM)] * 5,
        out_specs=pl.BlockSpec(memory_space=pltpu.VMEM),
        scratch_shapes=[
            pltpu.SMEM(mask.shape, jnp.int32),
            pltpu.SMEM(counts.shape, jnp.int32),
            pltpu.VMEM((lags, lags), jnp.bfloat16),
            pltpu.VMEM((lags, lags), jnp.bfloat16),
            pltpu.SemaphoreType.DMA((4,)),
            pltpu.VMEM((TEAM, wins, lags, LANES), jnp.bfloat16),
            pltpu.VMEM((SLOTS, wins, lags, LANES), jnp.bfloat16),
            pltpu.VMEM((PAIRS, lags, LANES), jnp.float32),
            pltpu.VMEM((2 * PAIRS, bins, LANES), jnp.bfloat16),
            pltpu.SemaphoreType.DMA((TEAM,)),
            pltpu.SemaphoreType.DMA((TEAM, groups)),
            pltpu.SemaphoreType.DMA((5,)),
            pltpu.SemaphoreType.DMA((5, groups)),
            pltpu.SemaphoreType.DMA((4,)),
            pltpu.SemaphoreType.DMA((2, MAXP)),
        ],
        compiler_params=pltpu.CompilerParams(collective_id=0, has_side_effects=True, vmem_limit_bytes=40 << 20),
        name="xcorr",
    )(*(pltpu.with_memory_space_constraint(x, pltpu.HBM) for x in (
        traces, mask, counts, jnp.asarray(table.T, jnp.bfloat16), jnp.asarray(table_lag, jnp.bfloat16))))
    wide = jax.ShapeDtypeStruct((1, MAXP, bins, width), jnp.float32)
    return pl.pallas_call(
        widen,
        out_shape=(wide, wide),
        in_specs=[pl.BlockSpec(memory_space=pltpu.VMEM)],
        out_specs=[pl.BlockSpec(memory_space=pltpu.HBM)] * 2,
        scratch_shapes=[
            pltpu.VMEM((2, MAXP, bins, width), jnp.float32),
            pltpu.SemaphoreType.DMA((2, MAXP)),
        ],
        name="widen",
    )(pltpu.with_memory_space_constraint(lagged, pltpu.VMEM))


def solution(mesh):
    return jax.shard_map(
        local,
        mesh=mesh,
        in_specs=(P(("grp", "chan"), None, None, None), P("grp", None), P("grp")),
        out_specs=(P(("grp", "chan"), None, None, None), P(("grp", "chan"), None, None, None)),
        check_vma=False,
    )
```

```python
import functools
import math

import numpy as np

import jax
import jax.numpy as jnp
from jax import lax
from jax.experimental import pallas as pl
from jax.experimental.pallas import tpu as pltpu
from jax.sharding import PartitionSpec as P

MAXP = 5
TEAM = 4
LANES = 128
CHUNK = 2
SLOTS = 11
TILE = 16
NEAR_LAG = 2
FAR_LAG = 2
AHEAD = 4
OWN, BELOW, ABOVE, BOTH = range(4)

SOON = [
    ("n0", "n1", OWN), ("n0", "f0", OWN), ("n1", "f0", OWN),
    (0, "n0", BELOW), (0, "n1", BELOW), (0, "f0", BELOW),
    ("n0", 6, ABOVE), ("n1", 6, ABOVE), ("f0", 6, ABOVE), ("x0", "x1", OWN),
]
FAR = [
    ("n0", "f1", OWN), ("n1", "f1", OWN), (0, "f1", BELOW), ("f1", 6, ABOVE),
]
LATE_A = [(1, "n0", BELOW), (1, "n1", BELOW), (1, "f0", BELOW), (1, "f1", BELOW), (1, 6, BOTH)]
LATE_B = [("n0", 7, ABOVE), ("n1", 7, ABOVE), ("f0", 7, ABOVE), ("f1", 7, ABOVE)]
LAST = [(3, 8, ABOVE), (4, 8, ABOVE), (5, 8, ABOVE)]
LISTS = (SOON, FAR, LATE_A, LATE_B, LAST)
PAIRS = sum(len(pairs) for pairs in LISTS)


def lag_table(lags, bins):
    times = np.arange(lags, dtype=np.int32)[:, None]
    freqs = np.arange(1, bins + 1, dtype=np.int32)[None, :]
    phase = (times * freqs % lags).astype(np.float32) * np.float32(2.0 * math.pi / lags)
    return np.concatenate([np.cos(phase), -np.sin(phase)], axis=1)


def kernel(axis, n, traces, mask_in, counts_in, table_t_in, table_lag_in, back,
           mask, counts, table_t, table_lag, fetch, record, white, acc, res,
           t_send, t_recv, z_send, z_recv, r_send, r_recv, entered):
    me = lax.axis_index(axis)
    team = me // TEAM
    q = me % TEAM
    base = team * TEAM
    odd = q % 2
    teams = n // TEAM
    wins = record.shape[1]
    lags = record.shape[2]
    bins = lags // 2
    groups = wins // CHUNK
    below = team > 0
    above = team < teams - 1
    step = TEAM * (1 - 2 * odd)
    has_a = jnp.where(odd == 0, team, teams - 1 - team) > 0
    has_b = jnp.where(odd == 0, teams - 1 - team, team) > 0
    low = (q % 3) == 0
    sign = (1 - 2 * odd).astype(jnp.float32)
    near_u = jnp.where(low, 0, 2)
    far_u = 2 - near_u
    slot_of = {"n0": near_u + 2, "n1": near_u + 3, "f0": far_u + 2, "f1": far_u + 3, "x0": 9, "x1": 10}

    def slot(name):
        return slot_of[name] if isinstance(name, str) else name

    def there(group):
        return {OWN: True, BELOW: has_a, ABOVE: has_b, BOTH: has_a & has_b}[group]

    def block_of(s):
        return base + jnp.where(odd == 0, s - 2, 5 - s)

    fetches = [
        pltpu.make_async_copy(src, dst, fetch.at[k])
        for k, (src, dst) in enumerate(
            ((table_t_in, table_t), (mask_in, mask), (table_lag_in, table_lag), (counts_in, counts)))
    ]
    barrier = pltpu.get_barrier_semaphore()
    for other in (me - TEAM, me + TEAM, base + (q + 2) % TEAM, base + 3 - q, me + 1 - 2 * odd):
        @pl.when((other >= 0) & (other < n))
        def _():
            pl.semaphore_signal(barrier, inc=1, device_id={axis: other})

    for copy in fetches:
        copy.start()

    def windows(g):
        return pl.ds(g * CHUNK, CHUNK)

    def lanes(i):
        return pl.ds(pl.multiple_of(i * LANES, LANES), LANES)

    def trace_copy(peer, at, extra=0):
        return lambda g: pltpu.make_async_remote_copy(
            src_ref=traces.at[0, at(g), :, lanes((peer + extra) % TEAM)],
            dst_ref=record.at[TEAM + odd if extra else q, at(g)],
            send_sem=t_send.at[TEAM if extra else peer],
            recv_sem=t_recv.at[TEAM + odd if extra else q, g],
            device_id={axis: base + peer},
        )

    def own_copy(g, extra=0):
        at = TEAM + odd if extra else q
        return pltpu.make_async_copy(
            traces.at[0, windows(g), :, lanes((q + extra) % TEAM)], record.at[at, windows(g)], t_recv.at[at, g])

    sibling = q + 1 - 2 * odd
    flows = (((q + 2) % TEAM, 0), (3 - q, 0), (sibling, 0), (sibling, 2))
    for g in range(groups):
        own_copy(g).start()

    def every(g):
        return pl.ds(0, wins)

    def to_a(u, g, at=windows):
        return pltpu.make_async_remote_copy(
            src_ref=white.at[u + 2, at(g)],
            dst_ref=white.at[u + 6, at(g)],
            send_sem=z_send.at[u],
            recv_sem=z_recv.at[u + 2, g],
            device_id={axis: me - step},
        )

    def to_b(u, g, at=windows):
        return pltpu.make_async_remote_copy(
            src_ref=white.at[u + 2, at(g)],
            dst_ref=white.at[u - 2, at(g)],
            send_sem=z_send.at[u + 1],
            recv_sem=z_recv.at[u - 2, g],
            device_id={axis: me + step},
        )

    def whiten_block(u, g):
        whiten(jnp.where(odd == 0, u, 3 - u), jnp.where(odd == 0, u, 3 - u), u + 2, g)

    def whiten(i, block, into, g):
        pltpu.make_async_copy(record.at[i, windows(g)], record.at[i, windows(g)], t_recv.at[i, g]).wait()
        w = g * CHUNK
        rec = jnp.concatenate([record[i, w + e] for e in range(CHUNK)], axis=1)
        raw = jnp.dot(table_t[...], rec, preferred_element_type=jnp.float32)
        power = jnp.sum(raw * raw, axis=0, keepdims=True) / bins
        inv = 1.0 / jnp.sqrt(power + 1e-06)
        for e in range(CHUNK):
            part = slice(e * LANES, (e + 1) * LANES)
            keep = mask[base + block, w + e].astype(jnp.float32)
            white[into, w + e] = (raw[:, part] * (inv[:, part] * keep)).astype(jnp.bfloat16)

    def send_a(u, g):
        @pl.when(has_a)
        def _():
            to_a(u, g).start()

    def send_b(u, g):
        @pl.when(has_b)
        def _():
            to_b(u, g).start()

    def arrived(z, g):
        view = white.at[z if z < 2 else z + 4, windows(g)]
        pltpu.make_async_copy(view, view, z_recv.at[z, g]).wait()

    place_of = {pair[:2]: k for k, pair in enumerate(sum(LISTS, []))}

    def stack(pairs, g):
        def tile(k, carry):
            re_at = pl.ds(pl.multiple_of(k * TILE, TILE), TILE)
            im_at = pl.ds(pl.multiple_of(bins + k * TILE, TILE), TILE)
            sums = [(acc[place_of[p[:2]], re_at, :], acc[place_of[p[:2]], im_at, :]) for p in pairs]
            for h in range(CHUNK):
                w = g * CHUNK + h
                names = list(dict.fromkeys(name for p in pairs for name in p[:2]))
                held = {
                    name: (white[slot(name), w, re_at, :].astype(jnp.float32), white[slot(name), w, im_at, :].astype(jnp.float32))
                    for name in names
                }
                for k2, p in enumerate(pairs):
                    a_re, a_im = held[p[0]]
                    b_re, b_im = held[p[1]]
                    real, imag = sums[k2]
                    sums[k2] = (real + (a_re * b_re + a_im * b_im), imag + (a_im * b_re - a_re * b_im))
            for k2, p in enumerate(pairs):
                acc[place_of[p[:2]], re_at, :] = sums[k2][0]
                acc[place_of[p[:2]], im_at, :] = sums[k2][1]
            return carry

        lax.fori_loop(0, bins // TILE, tile, 0, unroll=True)

    def result_copies(s, t, place, group, lane):
        early = block_of(jnp.where(odd == 0, s, t))
        late = block_of(jnp.where(odd == 0, t, s))
        out = []
        kept = ((s > 1) | (t > 4), (s < 4) | (t < 6))
        for side, owner, wanted in (
            (0, early, jnp.where(odd == 0, *kept)), (1, late, jnp.where(odd == 0, *kept[::-1]))):
            src = res.at[2 * place + side]
            dst = back.at[side, t - s - 1, :, lanes(lane)]
            local = pltpu.make_async_copy(src, dst, r_recv.at[side, t - s - 1])
            remote = pltpu.make_async_remote_copy(
                src_ref=src, dst_ref=dst, send_sem=r_send.at[group],
                recv_sem=r_recv.at[side, t - s - 1], device_id={axis: owner},
            )
            out.append((wanted, owner, local, remote))
        return early, out

    def finish(place, first, second, group):
        again = first == 9
        first = jnp.where(again, near_u + 2, first)
        second = jnp.where(again, near_u + 3, second)
        s = jnp.minimum(first, second)
        t = jnp.maximum(first, second)
        turn = jnp.where(first < second, sign, -sign)
        early, copies = result_copies(s, t, place, group, jnp.where(again, (q + 2) % TEAM, q))
        total = acc[place] * (1.0 / math.sqrt(wins))
        stacked = jnp.concatenate([total[:bins], total[bins:] * turn], axis=0).astype(jnp.bfloat16)
        corr = jnp.dot(table_lag[...], stacked, preferred_element_type=jnp.float32) * (1.0 / math.sqrt(bins))
        corr = jnp.where(counts[early] >= t - s, corr, 0.0).astype(jnp.bfloat16)
        res[2 * place] = corr[:bins]
        res[2 * place + 1] = corr[bins:]
        for wanted, owner, local, remote in copies:
            @pl.when(wanted & (owner == me))
            def _():
                local.start()

            @pl.when(wanted & (owner != me))
            def _():
                remote.start()

    def choose(k, values):
        out = values[0]
        for at, value in enumerate(values[1:], 1):
            out = jnp.where(k == at, value, out)
        return out

    def finish_one(k, pairs):
        ready = choose(k, [jnp.where(there(p[2]), 1, 0) for p in pairs]) > 0

        @pl.when(ready & (k < len(pairs)))
        def _():
            finish(place_of[pairs[0][:2]] + k, choose(k, [slot(p[0]) for p in pairs]),
                   choose(k, [slot(p[1]) for p in pairs]), choose(k, [p[2] for p in pairs]))

    def finish_all(pairs):
        def one(k, carry):
            finish_one(k, pairs)
            return carry

        lax.fori_loop(0, len(pairs), one, 0)

    for copy in fetches[:2]:
        copy.wait()
    own_u = near_u
    whiten_block(own_u, 0)
    sides = below.astype(jnp.int32) + above.astype(jnp.int32)
    pl.semaphore_wait(barrier, TEAM - 1 + sides)

    def start_own(g):
        @pl.when(low)
        def _():
            send_a(0, g)

        @pl.when(jnp.logical_not(low))
        def _():
            send_b(2, g)

            @pl.when(g < AHEAD)
            def _():
                send_a(2, g)

    for at, (peer, extra) in enumerate(flows):
        copy = trace_copy(peer, windows, extra)
        for g in range(groups):
            copy(g).start()
            if at == 0 and g == 0:
                start_own(0)
    for g in range(groups):
        own_copy(g, 2).start()

    def own_chunk(g, carry):
        whiten_block(own_u, g)
        start_own(g)
        return carry

    for other in (me - TEAM, me + TEAM):
        @pl.when((other >= 0) & (other < n))
        def _():
            pl.semaphore_signal(entered, inc=1, device_id={axis: other})

    lax.fori_loop(1, groups, own_chunk, 0)
    acc[...] = jnp.zeros_like(acc)
    for j in range(MAXP):
        for side, gone in ((0, me + j + 1 >= n), (1, me - j - 1 < 0)):
            @pl.when(gone)
            def _():
                back[side, j] = jnp.zeros_like(back[side, j])
    for copy in fetches[2:]:
        copy.wait()
    pl.semaphore_wait(entered, sides)

    def of(pairs, group):
        return [p for p in pairs if p[2] == group]

    def soon_a(g):
        arrived(0, g)
        stack(of(SOON, BELOW), g)

    def soon_b(g):
        arrived(2, g)
        stack(of(SOON, ABOVE), g)

    def late_a(g):
        arrived(1, g)
        stack(of(LATE_A, BELOW), g)

        @pl.when(has_b)
        def _():
            stack(of(LATE_A, BOTH), g)

    def late_b(g):
        arrived(3, g)
        stack(LATE_B, g)

    lag_a = jnp.where(low, FAR_LAG, NEAR_LAG)
    lag_b = jnp.where(low, NEAR_LAG, FAR_LAG)

    def one_step(k, carry):
        late = k >= groups
        g = jnp.where(late, k - groups, k)
        u = far_u + late.astype(jnp.int32)
        whiten_block(u, g)

        @pl.when(low)
        def _():
            send_b(u, g)

            @pl.when(late)
            def _():
                send_a(2, g)

        @pl.when(jnp.logical_not(low))
        def _():
            send_a(u, g)

            @pl.when(k == 2 * groups - 1)
            def _():
                for h in range(AHEAD, groups):
                    send_a(2, h)

        @pl.when(jnp.logical_not(late))
        def _():
            whiten_block(near_u + 1, g)

            @pl.when(low)
            def _():
                send_a(1, g)

            @pl.when(jnp.logical_not(low))
            def _():
                send_b(3, g)

            for e in range(2):
                u = near_u + e
                block = jnp.where(odd == 0, u, 3 - u)
                whiten(TEAM + block % 2, block, 9 + e, g)
            stack([p for p in of(SOON, OWN) if p[0] != "x0"], g)
            stack([p for p in of(SOON, OWN) if p[0] == "x0"], g)

        for lag, there_too, soon_part, late_part in ((lag_a, has_a, soon_a, late_a), (lag_b, has_b, soon_b, late_b)):
            h = k - lag

            @pl.when(there_too & (h >= 0) & (h < groups))
            def _():
                soon_part(h)

            @pl.when(there_too & (h >= groups))
            def _():
                late_part(h - groups)

        @pl.when(late)
        def _():
            stack(of(FAR, OWN), g)

            @pl.when(has_a)
            def _():
                stack(of(FAR, BELOW), g)

            @pl.when(has_b)
            def _():
                stack(of(FAR, ABOVE), g)

            for e in range(2):
                at = 2 * (g - FAR_LAG) + e

                @pl.when(at >= 0)
                def _():
                    finish_one(at, SOON)

        return carry

    lax.fori_loop(0, 2 * groups, one_step, 0)
    finish_all(FAR)

    def drain(p, carry):
        is_a = (p == 0) != low
        for mine, lag, there_too, late_part, pairs in (
            (is_a, lag_a, has_a, late_a, LATE_A), (jnp.logical_not(is_a), lag_b, has_b, late_b, LATE_B)):
            @pl.when(mine & there_too)
            def _():
                def one(g, inner):
                    late_part(g)
                    return inner

                lax.fori_loop(groups - lag, groups, one, 0)
                finish_all(pairs)

        return carry

    lax.fori_loop(0, 2, drain, 0)

    @pl.when(has_b)
    def _():
        def last(g, carry):
            arrived(4, g)
            stack(LAST, g)
            return carry

        lax.fori_loop(0, groups, last, 0)
        finish_all(LAST)

    for peer, extra in flows:
        trace_copy(peer, every, extra)(0).wait_send()

    @pl.when(has_a)
    def _():
        for u in range(3):
            to_a(u, 0, every).wait_send()

    @pl.when(has_b)
    def _():
        for u in range(2, 4):
            to_b(u, 0, every).wait_send()

    def results_sent(group, count, when):
        @pl.when(when)
        def _():
            view = res.at[pl.ds(0, count)]
            pltpu.make_async_copy(view, view, r_send.at[group]).wait()

    results_sent(OWN, 8, me >= 0)
    results_sent(BELOW, 8, has_a)
    results_sent(ABOVE, 14, has_b & low)
    results_sent(ABOVE, 13, has_b & jnp.logical_not(low))
    results_sent(BOTH, 2, has_a & has_b)
    for j in range(MAXP):
        for side, some in ((0, me + j + 1 < n), (1, me - j - 1 >= 0)):
            @pl.when(some)
            def _():
                view = back.at[side, j]
                pltpu.make_async_copy(view, view, r_recv.at[side, j]).wait()


def widen(back, fwd_out, bwd_out, wide, sems):
    copies = []
    for j in range(MAXP):
        for side, out in ((0, fwd_out), (1, bwd_out)):
            wide[side, j] = back[side, j].astype(jnp.float32)
            copy = pltpu.make_async_copy(wide.at[side, j], out.at[0, j], sems.at[side, j])
            copy.start()
            copies.append(copy)
    for copy in copies:
        copy.wait()


def local(traces, mask, counts):
    axis = "chan"
    n = lax.axis_size(axis)
    _, wins, lags, width = traces.shape
    bins = lags // 2
    groups = wins // CHUNK
    table = lag_table(lags, bins)
    table_lag = np.concatenate([table[:bins], table[bins:][::-1]], axis=0)
    lagged = pl.pallas_call(
        functools.partial(kernel, axis, n),
        out_shape=pltpu.VMEM((2, MAXP, bins, width), jnp.bfloat16),
        in_specs=[pl.BlockSpec(memory_space=pltpu.HBM)] * 5,
        out_specs=pl.BlockSpec(memory_space=pltpu.VMEM),
        scratch_shapes=[
            pltpu.SMEM(mask.shape, jnp.int32),
            pltpu.SMEM(counts.shape, jnp.int32),
            pltpu.VMEM((lags, lags), jnp.bfloat16),
            pltpu.VMEM((lags, lags), jnp.bfloat16),
            pltpu.SemaphoreType.DMA((4,)),
            pltpu.VMEM((TEAM + 2, wins, lags, LANES), jnp.bfloat16),
            pltpu.VMEM((SLOTS, wins, lags, LANES), jnp.bfloat16),
            pltpu.VMEM((PAIRS, lags, LANES), jnp.float32),
            pltpu.VMEM((2 * PAIRS, bins, LANES), jnp.bfloat16),
            pltpu.SemaphoreType.DMA((TEAM + 1,)),
            pltpu.SemaphoreType.DMA((TEAM + 2, groups)),
            pltpu.SemaphoreType.DMA((5,)),
            pltpu.SemaphoreType.DMA((5, groups)),
            pltpu.SemaphoreType.DMA((4,)),
            pltpu.SemaphoreType.DMA((2, MAXP)),
            pltpu.SemaphoreType.REGULAR,
        ],
        compiler_params=pltpu.CompilerParams(collective_id=0, has_side_effects=True, vmem_limit_bytes=40 << 20),
        name="xcorr",
    )(*(pltpu.with_memory_space_constraint(x, pltpu.HBM) for x in (
        traces, mask, counts, jnp.asarray(table.T, jnp.bfloat16), jnp.asarray(table_lag, jnp.bfloat16))))
    wide = jax.ShapeDtypeStruct((1, MAXP, bins, width), jnp.float32)
    return pl.pallas_call(
        widen,
        out_shape=(wide, wide),
        in_specs=[pl.BlockSpec(memory_space=pltpu.VMEM)],
        out_specs=[pl.BlockSpec(memory_space=pltpu.HBM)] * 2,
        scratch_shapes=[
            pltpu.VMEM((2, MAXP, bins, width), jnp.float32),
            pltpu.SemaphoreType.DMA((2, MAXP)),
        ],
        name="widen",
    )(pltpu.with_memory_space_constraint(lagged, pltpu.VMEM))


def solution(mesh):
    return jax.shard_map(
        local,
        mesh=mesh,
        in_specs=(P(("grp", "chan"), None, None, None), P("grp", None), P("grp")),
        out_specs=(P(("grp", "chan"), None, None, None), P(("grp", "chan"), None, None, None)),
        check_vma=False,
    )
```

```python
import functools
import math

import numpy as np

import jax
import jax.numpy as jnp
from jax import lax
from jax.experimental import pallas as pl
from jax.experimental.pallas import tpu as pltpu
from jax.sharding import PartitionSpec as P

MAXP = 5
TEAM = 4
LANES = 128
CHUNK = 2
SLOTS = 11
HOLD = 7
TILE = 16
NEAR_LAG = 2
FAR_LAG = 2
AHEAD = 5
OWN, BELOW, ABOVE, BOTH = range(4)

SOON = [
    ("n0", "n1", OWN), ("n0", "f0", OWN), ("n1", "f0", OWN),
    (0, "n0", BELOW), (0, "n1", BELOW), (0, "f0", BELOW),
    ("n0", 6, ABOVE), ("n1", 6, ABOVE), ("f0", 6, ABOVE), ("x0", "x1", OWN),
]
FAR = [
    ("n0", "f1", OWN), ("n1", "f1", OWN), (0, "f1", BELOW), ("f1", 6, ABOVE),
]
LATE_A = [(1, "n0", BELOW), (1, "n1", BELOW), (1, "f0", BELOW), (1, "f1", BELOW), (1, 6, BOTH)]
LATE_B = [("n0", 7, ABOVE), ("n1", 7, ABOVE), ("f0", 7, ABOVE), ("f1", 7, ABOVE)]
LAST = [(3, 8, ABOVE), (4, 8, ABOVE), (5, 8, ABOVE)]
LISTS = (SOON, FAR, LATE_A, LATE_B, LAST)
PAIRS = sum(len(pairs) for pairs in LISTS)


def lag_table(lags, bins):
    times = np.arange(lags, dtype=np.int32)[:, None]
    freqs = np.arange(1, bins + 1, dtype=np.int32)[None, :]
    phase = (times * freqs % lags).astype(np.float32) * np.float32(2.0 * math.pi / lags)
    return np.concatenate([np.cos(phase), -np.sin(phase)], axis=1)


def kernel(axis, n, traces, mask_in, counts_in, table_t_in, table_lag_in, back,
           mask, counts, table_t, table_lag, fetch, record, white, acc, res,
           t_send, t_recv, z_send, z_recv, r_send, r_recv, entered):
    me = lax.axis_index(axis)
    team = me // TEAM
    q = me % TEAM
    base = team * TEAM
    odd = q % 2
    teams = n // TEAM
    wins = record.shape[1]
    lags = record.shape[2]
    bins = lags // 2
    groups = wins // CHUNK
    below = team > 0
    above = team < teams - 1
    step = TEAM * (1 - 2 * odd)
    has_a = jnp.where(odd == 0, team, teams - 1 - team) > 0
    has_b = jnp.where(odd == 0, teams - 1 - team, team) > 0
    low = (q % 3) == 0
    sign = (1 - 2 * odd).astype(jnp.float32)
    near_u = jnp.where(low, 0, 2)
    far_u = 2 - near_u
    slot_of = {"n0": near_u + 2, "n1": near_u + 3, "f0": far_u + 2, "f1": far_u + 3, "x0": 9, "x1": 10}

    def slot(name):
        return slot_of[name] if isinstance(name, str) else name

    def there(group):
        return {OWN: True, BELOW: has_a, ABOVE: has_b, BOTH: has_a & has_b}[group]

    def block_of(s):
        return base + jnp.where(odd == 0, s - 2, 5 - s)

    fetches = [
        pltpu.make_async_copy(src, dst, fetch.at[k])
        for k, (src, dst) in enumerate(
            ((table_t_in, table_t), (mask_in, mask), (table_lag_in, table_lag), (counts_in, counts)))
    ]
    barrier = pltpu.get_barrier_semaphore()
    for other in (me - TEAM, me + TEAM, base + (q + 2) % TEAM, base + 3 - q, me + 1 - 2 * odd):
        @pl.when((other >= 0) & (other < n))
        def _():
            pl.semaphore_signal(barrier, inc=1, device_id={axis: other})

    for copy in fetches:
        copy.start()

    def windows(g):
        return pl.ds(g * CHUNK, CHUNK)

    def lanes(i):
        return pl.ds(pl.multiple_of(i * LANES, LANES), LANES)

    def trace_copy(peer, at, extra=0):
        return lambda g: pltpu.make_async_remote_copy(
            src_ref=traces.at[0, at(g), :, lanes((peer + extra) % TEAM)],
            dst_ref=record.at[TEAM + odd if extra else q, at(g)],
            send_sem=t_send.at[TEAM if extra else peer],
            recv_sem=t_recv.at[TEAM + odd if extra else q, g],
            device_id={axis: base + peer},
        )

    def own_copy(g, extra=0):
        at = TEAM + odd if extra else q
        return pltpu.make_async_copy(
            traces.at[0, windows(g), :, lanes((q + extra) % TEAM)], record.at[at, windows(g)], t_recv.at[at, g])

    sibling = q + 1 - 2 * odd
    flows = (((q + 2) % TEAM, 0), (3 - q, 0), (sibling, 0), (sibling, 2))
    for g in range(groups):
        own_copy(g).start()

    def every(g):
        return pl.ds(0, wins)

    def to_a(u, g, at=windows):
        return pltpu.make_async_remote_copy(
            src_ref=white.at[u + 2, at(g)],
            dst_ref=white.at[u + 6, at(g)],
            send_sem=z_send.at[u],
            recv_sem=z_recv.at[u + 2, g],
            device_id={axis: me - step},
        )

    def to_b(u, g, at=windows):
        return pltpu.make_async_remote_copy(
            src_ref=white.at[u + 2, at(g)],
            dst_ref=white.at[u - 2, at(g)],
            send_sem=z_send.at[u + 1],
            recv_sem=z_recv.at[u - 2, g],
            device_id={axis: me + step},
        )

    def whiten_block(u, g):
        whiten(jnp.where(odd == 0, u, 3 - u), jnp.where(odd == 0, u, 3 - u), u + 2, g)

    def whiten(i, block, into, g):
        pltpu.make_async_copy(record.at[i, windows(g)], record.at[i, windows(g)], t_recv.at[i, g]).wait()
        w = g * CHUNK
        rec = jnp.concatenate([record[i, w + e] for e in range(CHUNK)], axis=1)
        raw = jnp.dot(table_t[...], rec, preferred_element_type=jnp.float32)
        power = jnp.sum(raw * raw, axis=0, keepdims=True) / bins
        inv = 1.0 / jnp.sqrt(power + 1e-06)
        for e in range(CHUNK):
            part = slice(e * LANES, (e + 1) * LANES)
            keep = mask[base + block, w + e].astype(jnp.float32)
            white[into, w + e] = (raw[:, part] * (inv[:, part] * keep)).astype(jnp.bfloat16)

    def send_a(u, g):
        @pl.when(has_a)
        def _():
            to_a(u, g).start()

    def send_b(u, g):
        @pl.when(has_b)
        def _():
            to_b(u, g).start()

    def arrived(z, g):
        view = white.at[z if z < 2 else z + 4, windows(g)]
        pltpu.make_async_copy(view, view, z_recv.at[z, g]).wait()

    place_of = {pair[:2]: k for k, pair in enumerate(sum(LISTS, []))}

    def stack(pairs, g):
        def tile(k, carry):
            re_at = pl.ds(pl.multiple_of(k * TILE, TILE), TILE)
            im_at = pl.ds(pl.multiple_of(bins + k * TILE, TILE), TILE)
            sums = [(acc[place_of[p[:2]], re_at, :], acc[place_of[p[:2]], im_at, :]) for p in pairs]
            for h in range(CHUNK):
                w = g * CHUNK + h
                names = list(dict.fromkeys(name for p in pairs for name in p[:2]))
                held = {
                    name: (white[slot(name), w, re_at, :].astype(jnp.float32), white[slot(name), w, im_at, :].astype(jnp.float32))
                    for name in names
                }
                for k2, p in enumerate(pairs):
                    a_re, a_im = held[p[0]]
                    b_re, b_im = held[p[1]]
                    real, imag = sums[k2]
                    sums[k2] = (real + (a_re * b_re + a_im * b_im), imag + (a_im * b_re - a_re * b_im))
            for k2, p in enumerate(pairs):
                acc[place_of[p[:2]], re_at, :] = sums[k2][0]
                acc[place_of[p[:2]], im_at, :] = sums[k2][1]
            return carry

        lax.fori_loop(0, bins // TILE, tile, 0, unroll=True)

    def result_copies(s, t, place, group, lane):
        early = block_of(jnp.where(odd == 0, s, t))
        late = block_of(jnp.where(odd == 0, t, s))
        out = []
        kept = ((s > 1) | (t > 4), (s < 4) | (t < 6))
        for side, owner, wanted in (
            (0, early, jnp.where(odd == 0, *kept)), (1, late, jnp.where(odd == 0, *kept[::-1]))):
            src = res.at[2 * place + side]
            dst = back.at[side, t - s - 1, :, lanes(lane)]
            local = pltpu.make_async_copy(src, dst, r_recv.at[side, t - s - 1])
            remote = pltpu.make_async_remote_copy(
                src_ref=src, dst_ref=dst, send_sem=r_send.at[group],
                recv_sem=r_recv.at[side, t - s - 1], device_id={axis: owner},
            )
            out.append((wanted, owner, local, remote))
        return early, out

    def finish(place, first, second, group):
        again = first == 9
        first = jnp.where(again, near_u + 2, first)
        second = jnp.where(again, near_u + 3, second)
        s = jnp.minimum(first, second)
        t = jnp.maximum(first, second)
        turn = jnp.where(first < second, sign, -sign)
        early, copies = result_copies(s, t, place, group, jnp.where(again, (q + 2) % TEAM, q))
        total = acc[place] * (1.0 / math.sqrt(wins))
        stacked = jnp.concatenate([total[:bins], total[bins:] * turn], axis=0).astype(jnp.bfloat16)
        corr = jnp.dot(table_lag[...], stacked, preferred_element_type=jnp.float32) * (1.0 / math.sqrt(bins))
        corr = jnp.where(counts[early] >= t - s, corr, 0.0).astype(jnp.bfloat16)
        res[2 * place] = corr[:bins]
        res[2 * place + 1] = corr[bins:]
        for wanted, owner, local, remote in copies:
            @pl.when(wanted & (owner == me))
            def _():
                local.start()

            @pl.when(wanted & (owner != me) & (owner // TEAM == team))
            def _():
                remote.start()

    def cross(s, t, toward_s, group):
        places = {}
        for pair, place in place_of.items():
            if pair != ("x0", "x1"):
                places.setdefault(pair, place)

        def place_for(is_low):
            names = {"n0": 2, "n1": 3, "f0": 4, "f1": 5} if is_low else {"n0": 4, "n1": 5, "f0": 2, "f1": 3}
            for pair, place in places.items():
                if sorted(names.get(x, x) for x in pair) == [s, t]:
                    return place

        place = jnp.where(low, place_for(True), place_for(False))
        early, copies = result_copies(s, t, place, group, q)
        side = odd if toward_s else 1 - odd
        for k in range(2):
            @pl.when(there(group) & (side == k))
            def _():
                copies[k][3].start()

    def cross_all():
        for s, t, toward_s, group in (
            (0, 5, True, BELOW), (2, 6, False, ABOVE), (3, 6, False, ABOVE), (1, 5, True, BELOW),
            (2, 7, False, ABOVE), (3, 7, False, ABOVE), (1, 6, True, BOTH), (1, 6, False, BOTH)):
            cross(s, t, toward_s, group)

    def choose(k, values):
        out = values[0]
        for at, value in enumerate(values[1:], 1):
            out = jnp.where(k == at, value, out)
        return out

    def finish_one(k, pairs):
        ready = choose(k, [jnp.where(there(p[2]), 1, 0) for p in pairs]) > 0

        @pl.when(ready & (k < len(pairs)))
        def _():
            finish(place_of[pairs[0][:2]] + k, choose(k, [slot(p[0]) for p in pairs]),
                   choose(k, [slot(p[1]) for p in pairs]), choose(k, [p[2] for p in pairs]))

    def finish_all(pairs):
        def one(k, carry):
            finish_one(k, pairs)
            return carry

        lax.fori_loop(0, len(pairs), one, 0)

    for copy in fetches[:2]:
        copy.wait()
    own_u = near_u
    whiten_block(own_u, 0)
    sides = below.astype(jnp.int32) + above.astype(jnp.int32)
    pl.semaphore_wait(barrier, TEAM - 1 + sides)

    def start_own(g):
        @pl.when(low)
        def _():
            send_a(0, g)

        @pl.when(jnp.logical_not(low))
        def _():
            send_b(2, g)

            @pl.when(g < AHEAD)
            def _():
                send_a(2, g)

    for at, (peer, extra) in enumerate(flows):
        copy = trace_copy(peer, windows, extra)
        for g in range(groups):
            copy(g).start()
            if at == 0 and g == 0:
                start_own(0)
    for g in range(groups):
        own_copy(g, 2).start()

    def own_chunk(g, carry):
        whiten_block(own_u, g)
        start_own(g)
        return carry

    for other in (me - TEAM, me + TEAM):
        @pl.when((other >= 0) & (other < n))
        def _():
            pl.semaphore_signal(entered, inc=1, device_id={axis: other})

    lax.fori_loop(1, groups, own_chunk, 0)
    acc[...] = jnp.zeros_like(acc)
    for j in range(MAXP):
        for side, gone in ((0, me + j + 1 >= n), (1, me - j - 1 < 0)):
            @pl.when(gone)
            def _():
                back[side, j] = jnp.zeros_like(back[side, j])
    for copy in fetches[2:]:
        copy.wait()
    pl.semaphore_wait(entered, sides)

    def of(pairs, group):
        return [p for p in pairs if p[2] == group]

    def soon_a(g):
        arrived(0, g)
        stack(of(SOON, BELOW), g)

    def soon_b(g):
        arrived(2, g)
        stack(of(SOON, ABOVE), g)

    def late_a(g):
        arrived(1, g)
        stack(of(LATE_A, BELOW), g)

        @pl.when(has_b)
        def _():
            stack(of(LATE_A, BOTH), g)

    def late_b(g):
        arrived(3, g)
        stack(LATE_B, g)

    lag_a = jnp.where(low, FAR_LAG, NEAR_LAG)
    lag_b = jnp.where(low, NEAR_LAG, FAR_LAG)

    def one_step(k, carry):
        late = k >= groups
        g = jnp.where(late, k - groups, k)
        u = far_u + late.astype(jnp.int32)
        whiten_block(u, g)

        @pl.when(low)
        def _():
            send_b(u, g)

            @pl.when(late)
            def _():
                send_a(2, g)

        @pl.when(jnp.logical_not(low))
        def _():
            send_a(u, g)

            @pl.when(k == 2 * groups - 1)
            def _():
                for h in range(AHEAD, groups):
                    send_a(2, h)

        @pl.when(jnp.logical_not(late))
        def _():
            whiten_block(near_u + 1, g)

            @pl.when(low)
            def _():
                send_a(1, g)

            @pl.when(jnp.logical_not(low))
            def _():
                send_b(3, g)

            for e in range(2):
                u = near_u + e
                block = jnp.where(odd == 0, u, 3 - u)
                whiten(TEAM + block % 2, block, 9 + e, g)
            stack([p for p in of(SOON, OWN) if p[0] != "x0"], g)
            stack([p for p in of(SOON, OWN) if p[0] == "x0"], g)

        for lag, there_too, soon_part, late_part in ((lag_a, has_a, soon_a, late_a), (lag_b, has_b, soon_b, late_b)):
            h = k - lag

            @pl.when(there_too & (h >= 0) & (h < groups))
            def _():
                soon_part(h)

            @pl.when(there_too & (h >= groups))
            def _():
                late_part(h - groups)

        @pl.when(late)
        def _():
            stack(of(FAR, OWN), g)

            @pl.when(has_a)
            def _():
                stack(of(FAR, BELOW), g)

            @pl.when(has_b)
            def _():
                stack(of(FAR, ABOVE), g)

            for e in range(2):
                at = 2 * (g - FAR_LAG) + e

                @pl.when(at >= 0)
                def _():
                    finish_one(at, SOON)

        return carry

    lax.fori_loop(0, 2 * groups, one_step, 0)
    finish_all(FAR)

    def drain(p, carry):
        is_a = (p == 0) != low
        for mine, lag, there_too, late_part, pairs in (
            (is_a, lag_a, has_a, late_a, LATE_A), (jnp.logical_not(is_a), lag_b, has_b, late_b, LATE_B)):
            @pl.when(mine & there_too)
            def _():
                def one(g, inner):
                    late_part(g)
                    return inner

                lax.fori_loop(groups - lag, groups, one, 0)
                finish_all(pairs)

        return carry

    lax.fori_loop(0, 2, drain, 0)

    @pl.when(jnp.logical_not(has_b))
    def _():
        cross_all()

    @pl.when(has_b)
    def _():
        def last(g, carry):
            @pl.when(g == HOLD)
            def _():
                cross_all()

            arrived(4, g)
            stack(LAST, g)
            return carry

        lax.fori_loop(0, groups, last, 0)

        def finish_last(k, carry):
            finish_one(k, LAST)

            @pl.when(k == 0)
            def _():
                cross(3, 8, False, ABOVE)

            return carry

        lax.fori_loop(0, len(LAST), finish_last, 0)

    for peer, extra in flows:
        trace_copy(peer, every, extra)(0).wait_send()

    @pl.when(has_a)
    def _():
        for u in range(3):
            to_a(u, 0, every).wait_send()

    @pl.when(has_b)
    def _():
        for u in range(2, 4):
            to_b(u, 0, every).wait_send()

    def results_sent(group, count, when):
        @pl.when(when)
        def _():
            view = res.at[pl.ds(0, count)]
            pltpu.make_async_copy(view, view, r_send.at[group]).wait()

    results_sent(OWN, 8, me >= 0)
    results_sent(BELOW, 8, has_a)
    results_sent(ABOVE, 14, has_b & low)
    results_sent(ABOVE, 13, has_b & jnp.logical_not(low))
    results_sent(BOTH, 2, has_a & has_b)
    for j in range(MAXP):
        for side, some in ((0, me + j + 1 < n), (1, me - j - 1 >= 0)):
            @pl.when(some)
            def _():
                view = back.at[side, j]
                pltpu.make_async_copy(view, view, r_recv.at[side, j]).wait()


def widen(back, fwd_out, bwd_out, wide, sems):
    copies = []
    for j in range(MAXP):
        for side, out in ((0, fwd_out), (1, bwd_out)):
            wide[side, j] = back[side, j].astype(jnp.float32)
            copy = pltpu.make_async_copy(wide.at[side, j], out.at[0, j], sems.at[side, j])
            copy.start()
            copies.append(copy)
    for copy in copies:
        copy.wait()


def local(traces, mask, counts):
    axis = "chan"
    n = lax.axis_size(axis)
    _, wins, lags, width = traces.shape
    bins = lags // 2
    groups = wins // CHUNK
    table = lag_table(lags, bins)
    table_lag = np.concatenate([table[:bins], table[bins:][::-1]], axis=0)
    lagged = pl.pallas_call(
        functools.partial(kernel, axis, n),
        out_shape=pltpu.VMEM((2, MAXP, bins, width), jnp.bfloat16),
        in_specs=[pl.BlockSpec(memory_space=pltpu.HBM)] * 5,
        out_specs=pl.BlockSpec(memory_space=pltpu.VMEM),
        scratch_shapes=[
            pltpu.SMEM(mask.shape, jnp.int32),
            pltpu.SMEM(counts.shape, jnp.int32),
            pltpu.VMEM((lags, lags), jnp.bfloat16),
            pltpu.VMEM((lags, lags), jnp.bfloat16),
            pltpu.SemaphoreType.DMA((4,)),
            pltpu.VMEM((TEAM + 2, wins, lags, LANES), jnp.bfloat16),
            pltpu.VMEM((SLOTS, wins, lags, LANES), jnp.bfloat16),
            pltpu.VMEM((PAIRS, lags, LANES), jnp.float32),
            pltpu.VMEM((2 * PAIRS, bins, LANES), jnp.bfloat16),
            pltpu.SemaphoreType.DMA((TEAM + 1,)),
            pltpu.SemaphoreType.DMA((TEAM + 2, groups)),
            pltpu.SemaphoreType.DMA((5,)),
            pltpu.SemaphoreType.DMA((5, groups)),
            pltpu.SemaphoreType.DMA((4,)),
            pltpu.SemaphoreType.DMA((2, MAXP)),
            pltpu.SemaphoreType.REGULAR,
        ],
        compiler_params=pltpu.CompilerParams(collective_id=0, has_side_effects=True, vmem_limit_bytes=40 << 20),
        name="xcorr",
    )(*(pltpu.with_memory_space_constraint(x, pltpu.HBM) for x in (
        traces, mask, counts, jnp.asarray(table.T, jnp.bfloat16), jnp.asarray(table_lag, jnp.bfloat16))))
    wide = jax.ShapeDtypeStruct((1, MAXP, bins, width), jnp.float32)
    return pl.pallas_call(
        widen,
        out_shape=(wide, wide),
        in_specs=[pl.BlockSpec(memory_space=pltpu.VMEM)],
        out_specs=[pl.BlockSpec(memory_space=pltpu.HBM)] * 2,
        scratch_shapes=[
            pltpu.VMEM((2, MAXP, bins, width), jnp.float32),
            pltpu.SemaphoreType.DMA((2, MAXP)),
        ],
        name="widen",
    )(pltpu.with_memory_space_constraint(lagged, pltpu.VMEM))


def solution(mesh):
    return jax.shard_map(
        local,
        mesh=mesh,
        in_specs=(P(("grp", "chan"), None, None, None), P("grp", None), P("grp")),
        out_specs=(P(("grp", "chan"), None, None, None), P(("grp", "chan"), None, None, None)),
        check_vma=False,
    )
```

```python
import functools
import math

import numpy as np

import jax
import jax.numpy as jnp
from jax import lax
from jax.experimental import pallas as pl
from jax.experimental.pallas import tpu as pltpu
from jax.sharding import PartitionSpec as P

MAXP = 5
TEAM = 4
LANES = 128
CHUNK = 2
SLOTS = 11
HOLD = 7
FIRST = 3
EARLY = 2
TILE = 16
NEAR_LAG = 2
FAR_LAG = 2
AHEAD = 5
OWN, BELOW, ABOVE, BOTH = range(4)

SOON = [
    ("n0", "n1", OWN), ("n0", "f0", OWN), ("n1", "f0", OWN),
    (0, "n0", BELOW), (0, "n1", BELOW), (0, "f0", BELOW),
    ("n0", 6, ABOVE), ("n1", 6, ABOVE), ("f0", 6, ABOVE), ("x0", "x1", OWN),
]
FAR = [
    ("n0", "f1", OWN), ("n1", "f1", OWN), (0, "f1", BELOW), ("f1", 6, ABOVE),
]
LATE_A = [(1, "n0", BELOW), (1, "n1", BELOW), (1, "f0", BELOW), (1, "f1", BELOW), (1, 6, BOTH)]
LATE_B = [("n0", 7, ABOVE), ("n1", 7, ABOVE), ("f0", 7, ABOVE), ("f1", 7, ABOVE)]
LAST = [(3, 8, ABOVE), (4, 8, ABOVE), (5, 8, ABOVE)]
LISTS = (SOON, FAR, LATE_A, LATE_B, LAST)
PAIRS = sum(len(pairs) for pairs in LISTS)


def lag_table(lags, bins):
    times = np.arange(lags, dtype=np.int32)[:, None]
    freqs = np.arange(1, bins + 1, dtype=np.int32)[None, :]
    phase = (times * freqs % lags).astype(np.float32) * np.float32(2.0 * math.pi / lags)
    return np.concatenate([np.cos(phase), -np.sin(phase)], axis=1)


def kernel(axis, n, traces, mask_in, counts_in, table_t_in, table_lag_in, back,
           mask, counts, table_t, table_lag, fetch, record, white, acc, res,
           t_send, t_recv, z_send, z_recv, r_send, r_recv, entered, answer):
    me = lax.axis_index(axis)
    team = me // TEAM
    q = me % TEAM
    base = team * TEAM
    odd = q % 2
    teams = n // TEAM
    wins = record.shape[1]
    lags = record.shape[2]
    bins = lags // 2
    groups = wins // CHUNK
    below = team > 0
    above = team < teams - 1
    step = TEAM * (1 - 2 * odd)
    has_a = jnp.where(odd == 0, team, teams - 1 - team) > 0
    has_b = jnp.where(odd == 0, teams - 1 - team, team) > 0
    low = (q % 3) == 0
    sign = (1 - 2 * odd).astype(jnp.float32)
    near_u = jnp.where(low, 0, 2)
    far_u = 2 - near_u
    slot_of = {"n0": near_u + 2, "n1": near_u + 3, "f0": far_u + 2, "f1": far_u + 3, "x0": 9, "x1": 10}

    def slot(name):
        return slot_of[name] if isinstance(name, str) else name

    def there(group):
        return {OWN: True, BELOW: has_a, ABOVE: has_b, BOTH: has_a & has_b}[group]

    def block_of(s):
        return base + jnp.where(odd == 0, s - 2, 5 - s)

    fetches = [
        pltpu.make_async_copy(src, dst, fetch.at[k])
        for k, (src, dst) in enumerate(
            ((table_t_in, table_t), (mask_in, mask), (table_lag_in, table_lag), (counts_in, counts)))
    ]
    barrier = pltpu.get_barrier_semaphore()
    front = q < 2
    ahead = ((me - TEAM, 0, below), (base + (q + 2) % TEAM, 1, jnp.logical_not(front)),
             (base + 3 - q, 2, jnp.logical_not(front)), (me + 1 - 2 * odd, 3, odd == 1))
    behind = ((me + TEAM, 0, above), (base + (q + 2) % TEAM, 1, front), (base + 3 - q, 2, front),
              (me + 1 - 2 * odd, 3, odd == 0))
    for other, _, exists in behind:
        @pl.when(exists)
        def _():
            pl.semaphore_signal(barrier, inc=1, device_id={axis: other})

    for copy in fetches:
        copy.start()

    def windows(g):
        return pl.ds(g * CHUNK, CHUNK)

    def lanes(i):
        return pl.ds(pl.multiple_of(i * LANES, LANES), LANES)

    def trace_copy(peer, at, extra=0):
        return lambda g: pltpu.make_async_remote_copy(
            src_ref=traces.at[0, at(g), :, lanes((peer + extra) % TEAM)],
            dst_ref=record.at[TEAM + odd if extra else q, at(g)],
            send_sem=t_send.at[TEAM if extra else peer],
            recv_sem=t_recv.at[TEAM + odd if extra else q, g],
            device_id={axis: base + peer},
        )

    def own_copy(g, extra=0):
        at = TEAM + odd if extra else q
        return pltpu.make_async_copy(
            traces.at[0, windows(g), :, lanes((q + extra) % TEAM)], record.at[at, windows(g)], t_recv.at[at, g])

    sibling = q + 1 - 2 * odd
    flows = (((q + 2) % TEAM, 0), (3 - q, 0), (sibling, 0), (sibling, 2))
    for g in range(groups):
        own_copy(g).start()

    def every(g):
        return pl.ds(0, wins)

    def to_a(u, g, at=windows):
        return pltpu.make_async_remote_copy(
            src_ref=white.at[u + 2, at(g)],
            dst_ref=white.at[u + 6, at(g)],
            send_sem=z_send.at[u],
            recv_sem=z_recv.at[u + 2, g],
            device_id={axis: me - step},
        )

    def to_b(u, g, at=windows):
        return pltpu.make_async_remote_copy(
            src_ref=white.at[u + 2, at(g)],
            dst_ref=white.at[u - 2, at(g)],
            send_sem=z_send.at[u + 1],
            recv_sem=z_recv.at[u - 2, g],
            device_id={axis: me + step},
        )

    def whiten_block(u, g):
        whiten(jnp.where(odd == 0, u, 3 - u), jnp.where(odd == 0, u, 3 - u), u + 2, g)

    def whiten(i, block, into, g):
        pltpu.make_async_copy(record.at[i, windows(g)], record.at[i, windows(g)], t_recv.at[i, g]).wait()
        w = g * CHUNK
        rec = jnp.concatenate([record[i, w + e] for e in range(CHUNK)], axis=1)
        raw = jnp.dot(table_t[...], rec, preferred_element_type=jnp.float32)
        power = jnp.sum(raw * raw, axis=0, keepdims=True) / bins
        inv = 1.0 / jnp.sqrt(power + 1e-06)
        for e in range(CHUNK):
            part = slice(e * LANES, (e + 1) * LANES)
            keep = mask[base + block, w + e].astype(jnp.float32)
            white[into, w + e] = (raw[:, part] * (inv[:, part] * keep)).astype(jnp.bfloat16)

    def send_a(u, g, when=True):
        @pl.when(has_a & when)
        def _():
            to_a(u, g).start()

    def send_b(u, g, when=True):
        @pl.when(has_b & when)
        def _():
            to_b(u, g).start()

    def arrived(z, g):
        view = white.at[z if z < 2 else z + 4, windows(g)]
        pltpu.make_async_copy(view, view, z_recv.at[z, g]).wait()

    place_of = {pair[:2]: k for k, pair in enumerate(sum(LISTS, []))}

    def stack(pairs, g):
        def tile(k, carry):
            re_at = pl.ds(pl.multiple_of(k * TILE, TILE), TILE)
            im_at = pl.ds(pl.multiple_of(bins + k * TILE, TILE), TILE)
            sums = [(acc[place_of[p[:2]], re_at, :], acc[place_of[p[:2]], im_at, :]) for p in pairs]
            for h in range(CHUNK):
                w = g * CHUNK + h
                names = list(dict.fromkeys(name for p in pairs for name in p[:2]))
                held = {
                    name: (white[slot(name), w, re_at, :].astype(jnp.float32), white[slot(name), w, im_at, :].astype(jnp.float32))
                    for name in names
                }
                for k2, p in enumerate(pairs):
                    a_re, a_im = held[p[0]]
                    b_re, b_im = held[p[1]]
                    real, imag = sums[k2]
                    sums[k2] = (real + (a_re * b_re + a_im * b_im), imag + (a_im * b_re - a_re * b_im))
            for k2, p in enumerate(pairs):
                acc[place_of[p[:2]], re_at, :] = sums[k2][0]
                acc[place_of[p[:2]], im_at, :] = sums[k2][1]
            return carry

        lax.fori_loop(0, bins // TILE, tile, 0, unroll=True)

    def result_copies(s, t, place, group, lane):
        early = block_of(jnp.where(odd == 0, s, t))
        late = block_of(jnp.where(odd == 0, t, s))
        out = []
        kept = ((s > 1) | (t > 4), (s < 4) | (t < 6))
        for side, owner, wanted in (
            (0, early, jnp.where(odd == 0, *kept)), (1, late, jnp.where(odd == 0, *kept[::-1]))):
            src = res.at[2 * place + side]
            dst = back.at[side, t - s - 1, :, lanes(lane)]
            local = pltpu.make_async_copy(src, dst, r_recv.at[side, t - s - 1])
            remote = pltpu.make_async_remote_copy(
                src_ref=src, dst_ref=dst, send_sem=r_send.at[group],
                recv_sem=r_recv.at[side, t - s - 1], device_id={axis: owner},
            )
            out.append((wanted, owner, local, remote))
        return early, out

    def finish(place, first, second, group):
        again = first == 9
        first = jnp.where(again, near_u + 2, first)
        second = jnp.where(again, near_u + 3, second)
        s = jnp.minimum(first, second)
        t = jnp.maximum(first, second)
        turn = jnp.where(first < second, sign, -sign)
        early, copies = result_copies(s, t, place, group, jnp.where(again, (q + 2) % TEAM, q))
        total = acc[place] * (1.0 / math.sqrt(wins))
        stacked = jnp.concatenate([total[:bins], total[bins:] * turn], axis=0).astype(jnp.bfloat16)
        corr = jnp.dot(table_lag[...], stacked, preferred_element_type=jnp.float32) * (1.0 / math.sqrt(bins))
        corr = jnp.where(counts[early] >= t - s, corr, 0.0).astype(jnp.bfloat16)
        res[2 * place] = corr[:bins]
        res[2 * place + 1] = corr[bins:]
        for wanted, owner, local, remote in copies:
            @pl.when(wanted & (owner == me))
            def _():
                local.start()

            @pl.when(wanted & (owner != me) & (owner // TEAM == team))
            def _():
                remote.start()

    def cross(s, t, toward_s, group):
        places = {}
        for pair, place in place_of.items():
            if pair != ("x0", "x1"):
                places.setdefault(pair, place)

        def place_for(is_low):
            names = {"n0": 2, "n1": 3, "f0": 4, "f1": 5} if is_low else {"n0": 4, "n1": 5, "f0": 2, "f1": 3}
            for pair, place in places.items():
                if sorted(names.get(x, x) for x in pair) == [s, t]:
                    return place

        place = jnp.where(low, place_for(True), place_for(False))
        early, copies = result_copies(s, t, place, group, q)
        side = odd if toward_s else 1 - odd
        for k in range(2):
            @pl.when(there(group) & (side == k))
            def _():
                copies[k][3].start()

    def cross_some(part):
        for s, t, toward_s, group in (
            (0, 5, True, BELOW), (1, 5, True, BELOW), (1, 6, True, BOTH), (2, 6, False, ABOVE),
            (3, 6, False, ABOVE), (1, 6, False, BOTH), (2, 7, False, ABOVE), (3, 7, False, ABOVE))[part]:
            cross(s, t, toward_s, group)

    def choose(k, values):
        out = values[0]
        for at, value in enumerate(values[1:], 1):
            out = jnp.where(k == at, value, out)
        return out

    def finish_one(k, pairs):
        ready = choose(k, [jnp.where(there(p[2]), 1, 0) for p in pairs]) > 0

        @pl.when(ready & (k < len(pairs)))
        def _():
            finish(place_of[pairs[0][:2]] + k, choose(k, [slot(p[0]) for p in pairs]),
                   choose(k, [slot(p[1]) for p in pairs]), choose(k, [p[2] for p in pairs]))

    def finish_all(pairs):
        def one(k, carry):
            finish_one(k, pairs)
            return carry

        lax.fori_loop(0, len(pairs), one, 0)

    sides = below.astype(jnp.int32) + above.astype(jnp.int32)
    greetings = sum(exists.astype(jnp.int32) for _, _, exists in ahead)

    @pl.when(greetings > 0)
    def _():
        pl.semaphore_wait(barrier, greetings)

    for other, k, exists in ahead:
        @pl.when(exists)
        def _():
            pl.semaphore_signal(answer.at[k], inc=1, device_id={axis: other})

    for copy in fetches[:2]:
        copy.wait()
    own_u = near_u
    whiten_block(own_u, 0)
    def start_own(g, way_a=True, way_b=True):
        @pl.when(low)
        def _():
            send_a(0, g, way_a)

        @pl.when(jnp.logical_not(low))
        def _():
            send_b(2, g, way_b)

            @pl.when(g < AHEAD)
            def _():
                send_a(2, g, way_a)

    def answered(k):
        @pl.when(behind[k][2])
        def _():
            pl.semaphore_wait(answer.at[k], 1)

    def start_flow(peer, extra):
        copy = trace_copy(peer, windows, extra)
        for g in range(groups):
            copy(g).start()

    even = odd == 0
    start_own(0, even, odd == 1)

    @pl.when(jnp.logical_not(front))
    def _():
        start_flow(*flows[0])
        start_flow(*flows[1])

    for g in range(1, EARLY):
        whiten_block(own_u, g)
        start_own(g, even, odd == 1)

    @pl.when(front)
    def _():
        answered(1)
        start_flow(*flows[0])
        answered(2)
        start_flow(*flows[1])

    answered(0)
    for g in range(EARLY):
        start_own(g, odd == 1, even)
    answered(3)
    start_flow(*flows[2])
    start_flow(*flows[3])
    for g in range(groups):
        own_copy(g, 2).start()

    def own_chunk(g, carry):
        whiten_block(own_u, g)
        start_own(g)
        return carry

    for other in (me - TEAM, me + TEAM):
        @pl.when((other >= 0) & (other < n))
        def _():
            pl.semaphore_signal(entered, inc=1, device_id={axis: other})

    lax.fori_loop(EARLY, groups, own_chunk, 0)
    acc[...] = jnp.zeros_like(acc)
    for j in range(MAXP):
        for side, gone in ((0, me + j + 1 >= n), (1, me - j - 1 < 0)):
            @pl.when(gone)
            def _():
                back[side, j] = jnp.zeros_like(back[side, j])
    for copy in fetches[2:]:
        copy.wait()
    pl.semaphore_wait(entered, sides)

    def of(pairs, group):
        return [p for p in pairs if p[2] == group]

    def soon_a(g):
        arrived(0, g)
        stack(of(SOON, BELOW), g)

    def soon_b(g):
        arrived(2, g)
        stack(of(SOON, ABOVE), g)

    def late_a(g):
        arrived(1, g)
        stack(of(LATE_A, BELOW), g)

        @pl.when(has_b)
        def _():
            stack(of(LATE_A, BOTH), g)

    def late_b(g):
        arrived(3, g)
        stack(LATE_B, g)

    lag_a = jnp.where(low, FAR_LAG, NEAR_LAG)
    lag_b = jnp.where(low, NEAR_LAG, FAR_LAG)

    defer = odd == 1

    def one_step(k, carry):
        late = k >= groups
        g = jnp.where(late, k - groups, k)
        u = far_u + late.astype(jnp.int32)
        whiten_block(u, g)

        @pl.when(low)
        def _():
            send_b(u, g)

            @pl.when(late)
            def _():
                send_a(2, g)

        @pl.when(jnp.logical_not(low))
        def _():
            send_a(u, g)

            @pl.when(k == 2 * groups - 1)
            def _():
                for h in range(AHEAD, groups):
                    send_a(2, h)

        @pl.when(jnp.logical_not(late))
        def _():
            whiten_block(near_u + 1, g)

            @pl.when(low)
            def _():
                send_a(1, g)

            @pl.when(jnp.logical_not(low))
            def _():
                send_b(3, g)

            for e in range(2):
                u = near_u + e
                block = jnp.where(odd == 0, u, 3 - u)
                whiten(TEAM + block % 2, block, 9 + e, g)
            stack([p for p in of(SOON, OWN) if p[0] != "x0"], g)
            stack([p for p in of(SOON, OWN) if p[0] == "x0"], g)

        for lag, there_too, soon_part, late_part in ((lag_a, has_a, soon_a, late_a), (lag_b, has_b, soon_b, late_b)):
            h = k - lag

            @pl.when(there_too & (h >= 0) & (h < groups))
            def _():
                soon_part(h)

            @pl.when(there_too & (h >= groups))
            def _():
                late_part(h - groups)

        @pl.when(late)
        def _():
            stack(of(FAR, OWN), g)

            @pl.when(has_a)
            def _():
                stack(of(FAR, BELOW), g)

            @pl.when(has_b)
            def _():
                stack(of(FAR, ABOVE), g)

            for e in range(2):
                at = 2 * (g - FAR_LAG) + e

                @pl.when(at >= 0)
                def _():
                    finish_one(at, SOON)

        return carry

    lax.fori_loop(0, 2 * groups, one_step, 0)
    finish_all(FAR)

    def drain(p, carry):
        is_a = (p == 0) != low
        for mine, lag, there_too, late_part, pairs in (
            (is_a, lag_a, has_a, late_a, LATE_A), (jnp.logical_not(is_a), lag_b, has_b, late_b, LATE_B)):
            @pl.when(mine & there_too)
            def _():
                def one(g, inner):
                    late_part(g)
                    return inner

                lax.fori_loop(groups - lag, groups, one, 0)
                finish_all(pairs)

        return carry

    lax.fori_loop(0, 2, drain, 0)

    @pl.when(jnp.logical_not(has_b))
    def _():
        cross_some(slice(None))

    @pl.when(has_b)
    def _():
        def last(g, carry):
            @pl.when(g == HOLD - 1 + odd)
            def _():
                cross_some(slice(FIRST))

                @pl.when(jnp.logical_not(defer))
                def _():
                    cross_some(slice(FIRST, None))

            arrived(4, g)
            stack(LAST, g)
            return carry

        lax.fori_loop(0, groups, last, 0)

        def finish_last(k, carry):
            finish_one(k, LAST)

            @pl.when(k == 0)
            def _():
                cross(3, 8, False, ABOVE)

                @pl.when(defer)
                def _():
                    cross_some(slice(FIRST, None))

            return carry

        lax.fori_loop(0, len(LAST), finish_last, 0)

    for peer, extra in flows:
        trace_copy(peer, every, extra)(0).wait_send()

    @pl.when(has_a)
    def _():
        for u in range(3):
            to_a(u, 0, every).wait_send()

    @pl.when(has_b)
    def _():
        for u in range(2, 4):
            to_b(u, 0, every).wait_send()

    def results_sent(group, count, when):
        @pl.when(when)
        def _():
            view = res.at[pl.ds(0, count)]
            pltpu.make_async_copy(view, view, r_send.at[group]).wait()

    results_sent(OWN, 8, me >= 0)
    results_sent(BELOW, 8, has_a)
    results_sent(ABOVE, 14, has_b & low)
    results_sent(ABOVE, 13, has_b & jnp.logical_not(low))
    results_sent(BOTH, 2, has_a & has_b)
    for j in range(MAXP):
        for side, some in ((0, me + j + 1 < n), (1, me - j - 1 >= 0)):
            @pl.when(some)
            def _():
                view = back.at[side, j]
                pltpu.make_async_copy(view, view, r_recv.at[side, j]).wait()


def widen(back, fwd_out, bwd_out, wide, sems):
    copies = []
    for j in range(MAXP):
        for side, out in ((0, fwd_out), (1, bwd_out)):
            wide[side, j] = back[side, j].astype(jnp.float32)
            copy = pltpu.make_async_copy(wide.at[side, j], out.at[0, j], sems.at[side, j])
            copy.start()
            copies.append(copy)
    for copy in copies:
        copy.wait()


def local(traces, mask, counts):
    axis = "chan"
    n = lax.axis_size(axis)
    _, wins, lags, width = traces.shape
    bins = lags // 2
    groups = wins // CHUNK
    table = lag_table(lags, bins)
    table_lag = np.concatenate([table[:bins], table[bins:][::-1]], axis=0)
    lagged = pl.pallas_call(
        functools.partial(kernel, axis, n),
        out_shape=pltpu.VMEM((2, MAXP, bins, width), jnp.bfloat16),
        in_specs=[pl.BlockSpec(memory_space=pltpu.HBM)] * 5,
        out_specs=pl.BlockSpec(memory_space=pltpu.VMEM),
        scratch_shapes=[
            pltpu.SMEM(mask.shape, jnp.int32),
            pltpu.SMEM(counts.shape, jnp.int32),
            pltpu.VMEM((lags, lags), jnp.bfloat16),
            pltpu.VMEM((lags, lags), jnp.bfloat16),
            pltpu.SemaphoreType.DMA((4,)),
            pltpu.VMEM((TEAM + 2, wins, lags, LANES), jnp.bfloat16),
            pltpu.VMEM((SLOTS, wins, lags, LANES), jnp.bfloat16),
            pltpu.VMEM((PAIRS, lags, LANES), jnp.float32),
            pltpu.VMEM((2 * PAIRS, bins, LANES), jnp.bfloat16),
            pltpu.SemaphoreType.DMA((TEAM + 1,)),
            pltpu.SemaphoreType.DMA((TEAM + 2, groups)),
            pltpu.SemaphoreType.DMA((5,)),
            pltpu.SemaphoreType.DMA((5, groups)),
            pltpu.SemaphoreType.DMA((4,)),
            pltpu.SemaphoreType.DMA((2, MAXP)),
            pltpu.SemaphoreType.REGULAR,
            pltpu.SemaphoreType.REGULAR((4,)),
        ],
        compiler_params=pltpu.CompilerParams(collective_id=0, has_side_effects=True, vmem_limit_bytes=40 << 20),
        name="xcorr",
    )(*(pltpu.with_memory_space_constraint(x, pltpu.HBM) for x in (
        traces, mask, counts, jnp.asarray(table.T, jnp.bfloat16), jnp.asarray(table_lag, jnp.bfloat16))))
    wide = jax.ShapeDtypeStruct((1, MAXP, bins, width), jnp.float32)
    return pl.pallas_call(
        widen,
        out_shape=(wide, wide),
        in_specs=[pl.BlockSpec(memory_space=pltpu.VMEM)],
        out_specs=[pl.BlockSpec(memory_space=pltpu.HBM)] * 2,
        scratch_shapes=[
            pltpu.VMEM((2, MAXP, bins, width), jnp.float32),
            pltpu.SemaphoreType.DMA((2, MAXP)),
        ],
        name="widen",
    )(pltpu.with_memory_space_constraint(lagged, pltpu.VMEM))


def solution(mesh):
    return jax.shard_map(
        local,
        mesh=mesh,
        in_specs=(P(("grp", "chan"), None, None, None), P("grp", None), P("grp")),
        out_specs=(P(("grp", "chan"), None, None, None), P(("grp", "chan"), None, None, None)),
        check_vma=False,
    )
```
